32 devices in a mesh: expert: 8 (over z, y), dp: 4 (over x, core).
Axes of the slice: x: 2, y: 2, z: 4, core: 2. Of those that a mesh axis runs over, the one named last changes fastest.
Arguments:
- tokens: bfloat16 [4096, 1024], P(('expert', 'dp')), may hold values from -6 to 6
- routes: int32 [4096, 2], P(('expert', 'dp')), may hold values from 0 to 63, all different within a row; in each aligned block of 128 rows (0 to 127, 128 to 255, ...) at most 6 rows name the same one
- gate_values: float32 [4096, 2], P(('expert', 'dp')), may hold values from 0.02 to 0.5
- cotangent: bfloat16 [4096, 1024], P(('expert', 'dp')), may hold values from -6 to 6
- gating_weight: bfloat16 [64, 1024, 384], P('expert', 'dp'), may hold values from -0.1875 to 0.1875
- upward_weight: bfloat16 [64, 1024, 384], P('expert', 'dp'), may hold values from -0.1875 to 0.1875
- down_weight: bfloat16 [64, 1024, 384], P('expert', 'dp'), may hold values from -0.3125 to 0.3125
Outputs:
- layer_output: bfloat16 [4096, 1024], P(('expert', 'dp'))
- input_grad: bfloat16 [4096, 1024], P(('expert', 'dp'))
- gating_grad: float32 [64, 1024, 384], P('expert', 'dp')
- upward_grad: float32 [64, 1024, 384], P('expert', 'dp')
- down_grad: float32 [64, 1024, 384], P('expert', 'dp')
The draws below stay inside these ranges and needn't reach their ends.
Inputs may be any that keep to these rules, and one draw needn't show every extreme that they name: `routes`: each row names 2 different experts. Among the rows of one device no expert is named more than 6 times, and in every draw some device names some expert exactly 6 times.
All inputs are finite; a program needn't handle non-finite values.
Results may differ from the reference program's by a relative error of at most 0.017.
Values may be sent and summed in bfloat16 or wider, within the bound.
A program may use at most 128 MiB of HBM per device.

```python
import math
import jax
import jax.numpy as jnp
import numpy as np
from jax import lax

D = 1024
FF = 384
EXPERTS = 64
TOPK = 2
TOK_DEV = 128
CAP = 6
SHARDS = 4
TOKENS = 4096
N_EXPERT = 8


def shard_levels(stream_key, dims, cuts, low, top_value):
    factor_of, own = 1.0, jax.random.fold_in(stream_key, 6)
    for dim, shards_of in cuts:
        heights = jnp.exp(jax.random.uniform(jax.random.fold_in(own, dim), (shards_of,), jnp.float32, low / len(cuts), top_value / len(cuts)))
        factor_of = factor_of * jnp.repeat(heights, dims[dim] // shards_of).reshape([-1 if axis == dim else 1 for axis in range(len(dims))])
    return factor_of


def deal_out(stream_key, own, number, rows, amount, top, reach, lean):
    order = jax.random.permutation(stream_key, amount)
    crowded, usual = load_shares(amount, rows * top, reach, lean, True), load_shares(amount, rows * top, reach, lean, False)
    places = jnp.arange(amount)

    def named(sizes, offset_by):
        used = int((sizes > 0).sum())
        fixed = max(1, used // 4)
        passed = fixed + (places - fixed + offset_by * (used - fixed)) % max(1, amount - fixed)
        return jnp.zeros((amount,), jnp.int32).at[order[jnp.where(places < fixed, places, passed)]].set(jnp.asarray(sizes, jnp.int32))

    sizes = jnp.where(number % 4 == 0, named(crowded, number // 4), named(usual, number - number // 4 - 1))
    mixed = jax.random.permutation(jax.random.fold_in(own, 3), amount)
    source_of, receiver = mixed[0:amount // 2 * 2:2], mixed[1:amount // 2 * 2:2]
    slack = jnp.minimum(sizes[source_of] - 1, reach - sizes[receiver]) // 2
    slack = jnp.where((source_of == order[0]) | (receiver == order[0]) | (sizes[receiver] == 0), 0, jnp.maximum(slack, 0))
    passed = jax.random.randint(jax.random.fold_in(own, 4), (amount // 2,), 0, 1 << 20) % (slack + 1)
    sizes = sizes.at[source_of].add(-passed).at[receiver].add(passed)
    items = jnp.searchsorted(jnp.cumsum(sizes), jnp.arange(rows * top), side="right").astype(jnp.int32)
    listing = items.reshape(top, rows).T
    listing = listing[jax.random.permutation(jax.random.fold_in(own, 1), rows)]
    offset_by = jax.random.randint(jax.random.fold_in(own, 2), (rows, 1), 0, top)
    return jnp.take_along_axis(listing, (jnp.arange(top)[None, :] + offset_by) % top, axis=1)


def load_shares(count, total, bound, slope, full):
    weights = [(1 << 20) // math.isqrt(rank ** slope) + 1 for rank in range(1, count + 1)]
    largest = bound if full else min(bound, max(-(-total // count), total * weights[0] // sum(weights)))
    least = 1 if total - largest >= count - 1 else 0
    holding, surplus = [largest] + [least] * (count - 1), total - largest - least * (count - 1)
    while surplus > 0:
        movable = [i for i in range(1, count) if holding[i] < largest] or [i for i in range(1, count) if holding[i] < bound]
        whole, left = sum([weights[i] for i in movable]), surplus
        for i in movable:
            addition = min(bound - holding[i], max(1, left * weights[i] // whole), surplus)
            holding[i] = holding[i] + addition
            surplus = surplus - addition
    return np.array(holding)


def bell_draw(own_key, dims, spread, most, pieces=(), held_as=jnp.bfloat16):
    array = spread * jax.random.normal(own_key, dims, jnp.float32)
    if pieces:
        array = array * shard_levels(own_key, dims, pieces, -0.22, 0.18)
    return jnp.clip(array, -most, most).astype(held_as)


def setup_inputs(seed: int = 0) -> dict:
    splits = jax.random.split(jax.random.key(seed), 8)
    tokens = bell_draw(splits[0], (TOKENS, D), 1.0, 6.0, ((0, 32),))
    routes_keys = jax.random.split(jax.random.fold_in(splits[1], 1), TOKENS // TOK_DEV)
    routes_turns = jax.random.permutation(jax.random.fold_in(splits[1], 3), TOKENS // TOK_DEV)
    routes = jax.vmap(lambda own, number: deal_out(jax.random.fold_in(splits[1], 2), own, number, TOK_DEV, EXPERTS, TOPK, CAP, 2))(routes_keys, routes_turns).reshape((TOKENS, TOPK))
    gate_values = jnp.clip(jnp.exp(math.log(0.5) - 3.218876 * jax.random.uniform(splits[2], (TOKENS, TOPK), jnp.float32) ** shard_levels(splits[2], (TOKENS, TOPK), ((0, 32),), -0.2, 0.2)), 0.02, 0.5)
    cotangent = bell_draw(splits[3], (TOKENS, D), 1.0, 6.0, ((0, 32),))
    gating_weight = bell_draw(splits[4], (EXPERTS, D, FF), D ** -0.5, 0.1875, ((0, 8), (1, 4)))
    upward_weight = bell_draw(splits[5], (EXPERTS, D, FF), D ** -0.5, 0.1875, ((0, 8), (1, 4)))
    down_weight = bell_draw(splits[6], (EXPERTS, D, FF), FF ** -0.5, 0.3125, ((0, 8), (1, 4)))
    return {"tokens": tokens, "routes": routes, "gate_values": gate_values, "cotangent": cotangent, "gating_weight": gating_weight, "upward_weight": upward_weight, "down_weight": down_weight}


def reference(tokens, routes, gate_values, cotangent, gating_weight, upward_weight, down_weight):
    blocks = TOKENS // TOK_DEV
    pair_total = TOK_DEV * TOPK
    grouped = routes.reshape(blocks, pair_total)
    expert_ids = jnp.arange(EXPERTS, dtype=jnp.int32)
    onehot = (grouped[:, :, None] == expert_ids[None, None, :]).astype(jnp.int32)
    before = (jnp.cumsum(onehot, axis=1).astype(jnp.int32) - onehot).astype(jnp.int32)
    position = jnp.sum(before * onehot, axis=2).astype(jnp.int32)
    block_ids = jnp.broadcast_to(jnp.arange(blocks, dtype=jnp.int32)[:, None], (blocks, pair_total))
    pair_ids = (block_ids * pair_total + jnp.arange(pair_total, dtype=jnp.int32)[None, :]).astype(jnp.int32)
    slot_table = jnp.full((EXPERTS, blocks, CAP), -1, jnp.int32).at[grouped, block_ids, position].set(pair_ids)
    flat_gates = gate_values.reshape(-1)
    contract_last = (((1,), (1,)), ((), ()))

    def partial_sum(former, latter):
        first_rows = former.reshape(N_EXPERT, SHARDS, CAP, former.shape[-1]).astype(jnp.float32)
        second_rows = latter.reshape(N_EXPERT, SHARDS, CAP, latter.shape[-1]).astype(jnp.float32)
        block_sums = jnp.einsum("ajcd,ajcf->jdf", first_rows, second_rows, precision=lax.Precision.HIGHEST)
        rounded = lax.optimization_barrier(block_sums.astype(jnp.bfloat16))
        return jnp.sum(rounded.astype(jnp.float32), axis=0)

    def expert_step(carry, inputs):
        out_sum, grad_sum = carry
        slot_ids, gating, upward, lowering = inputs
        is_valid = (slot_ids >= 0).reshape(-1)
        safe_ids = jnp.maximum(slot_ids, 0).reshape(-1)
        token_ids = (safe_ids // TOPK).astype(jnp.int32)
        pair_weight = jnp.where(is_valid, flat_gates[safe_ids], jnp.zeros((), jnp.float32))
        expert_rows = jnp.where(is_valid[:, None], tokens[token_ids], jnp.zeros((), tokens.dtype))
        out_grad = (cotangent[token_ids].astype(jnp.float32) * pair_weight[:, None]).astype(jnp.bfloat16)
        gate_pre = jnp.dot(expert_rows, gating, preferred_element_type=jnp.float32)
        up_pre = jnp.dot(expert_rows, upward, preferred_element_type=jnp.float32)
        sigmoid_gate = jax.nn.sigmoid(gate_pre)
        activated = gate_pre * sigmoid_gate
        hidden = (activated * up_pre).astype(jnp.bfloat16)
        expert_out = lax.dot_general(hidden, lowering, contract_last, preferred_element_type=jnp.float32).astype(jnp.bfloat16)
        hidden_grad = jnp.dot(out_grad, lowering, preferred_element_type=jnp.float32)
        gate_part = (hidden_grad * up_pre * sigmoid_gate * (1.0 + gate_pre * (1.0 - sigmoid_gate))).astype(jnp.bfloat16)
        up_part = (hidden_grad * activated).astype(jnp.bfloat16)
        pair_grad = (lax.dot_general(gate_part, gating, contract_last, preferred_element_type=jnp.float32)
                     + lax.dot_general(up_part, upward, contract_last, preferred_element_type=jnp.float32)).astype(jnp.bfloat16)
        out_sum = out_sum.at[token_ids].add(pair_weight[:, None] * expert_out.astype(jnp.float32))
        grad_sum = grad_sum.at[token_ids].add(pair_grad.astype(jnp.float32))
        grads = (partial_sum(expert_rows, gate_part), partial_sum(expert_rows, up_part), partial_sum(out_grad, hidden))
        return (out_sum, grad_sum), grads

    zero_rows = jnp.zeros((TOKENS, D), jnp.float32)
    (out_sum, grad_sum), (gating_grad, upward_grad, down_grad) = lax.scan(
        expert_step, (zero_rows, zero_rows), (slot_table, gating_weight, upward_weight, down_weight))
    return (out_sum.astype(jnp.bfloat16), grad_sum.astype(jnp.bfloat16), gating_grad, upward_grad, down_grad)
```

```python
import functools
import jax
import jax.numpy as jnp
import numpy as np
from jax import lax
from jax.experimental import pallas as pl
from jax.experimental.pallas import tpu as pltpu
from jax.sharding import PartitionSpec as P

TOPK = 2
CAP = 6
MESH = pl.DeviceIdType.MESH
F32 = jnp.float32
BF16 = jnp.bfloat16


def plane_kernel(
    n_expert, n_dp, el, width,
    tok_in, cot_in, routes_in, gates_in, perm_in, back_in, wg_ref, wu_ref, wd_ref,
    layer_ref, igrad_ref, dg, du, dd,
    tok_ref, cot_ref, routes_ref, gates_ref, perm_ref, back_ref,
    wg, wu, wd, halves, meta, send, recv, rows, psend, pown, crecv, xsend, xrecv, hid,
    pre_ret, ret_send, ret, fin_send, fin_recv,
    in_send, in_recv, out_send, out_recv, pair_sem, swap_sem, local_sem,
):
    e_me = lax.axis_index("expert")
    d_me = lax.axis_index("dp")
    z_me, y_me = e_me // 2, lax.rem(e_me, 2)
    zh_me, zl_me = z_me // 2, lax.rem(z_me, 2)
    x_me, c_me = d_me // 2, lax.rem(d_me, 2)
    n_zh = n_expert // 4
    core_peer = (e_me, x_me * 2 + 1 - c_me)
    far_peer = (e_me, (1 - x_me) * 2 + c_me)
    per = n_zh * n_dp
    msg = el * CAP
    part = per * CAP
    half = el // 2
    ff = wg.shape[2]
    row_count = tok_ref.shape[0]
    slot_total = n_expert * msg
    wide = 2 * width
    plane = n_expert * 2

    def cols(index, size):
        return pl.ds(pl.multiple_of(index * size, size), size)

    def band(e):
        return pl.ds(pl.multiple_of(e * msg, msg), msg)

    input_copies = [
        pltpu.make_async_copy(src, dst, local_sem.at[5 + i])
        for i, (src, dst) in enumerate(
            (
                (routes_in, routes_ref), (gates_in, gates_ref), (tok_in, tok_ref), (cot_in, cot_ref),
                (perm_in, perm_ref), (back_in, back_ref),
            )
        )
    ]
    barrier = pltpu.get_barrier_semaphore()

    def greet(off, carry):
        other = lax.rem(e_me * 2 + c_me + off, plane)
        pl.semaphore_signal(
            barrier, inc=1, device_id=(other // 2, x_me * 2 + lax.rem(other, 2)), device_id_type=MESH
        )
        return carry

    lax.fori_loop(1, plane, greet, 0)
    pl.semaphore_signal(barrier, inc=1, device_id=far_peer, device_id_type=MESH)
    weight_copies = [
        pltpu.make_async_copy(src, dst, local_sem.at[i])
        for i, (src, dst) in enumerate(((wg_ref, wg), (wu_ref, wu), (wd_ref, wd)))
    ]
    for copy in input_copies:
        copy.start()
    for copy in weight_copies:
        copy.start()
    for copy in input_copies[:4]:
        copy.wait()

    expert_ids = lax.broadcasted_iota(jnp.int32, (n_expert * el, row_count), 0)
    named = [expert_ids == routes_ref[k : k + 1, :] for k in range(TOPK)]
    either = sum(jnp.where(n, 1.0, 0.0) for n in named).astype(BF16)
    square = (row_count, row_count)
    row_ids, col_ids = lax.broadcasted_iota(jnp.int32, square, 0), lax.broadcasted_iota(jnp.int32, square, 1)
    earlier = jnp.where(row_ids < col_ids, 1.0, 0.0).astype(BF16)
    before = jnp.dot(either, earlier, preferred_element_type=F32)
    for k in range(TOPK):
        position = jnp.sum(jnp.where(named[k], before, 0.0), axis=0, keepdims=True)
        meta[0, k : k + 1, :] = routes_ref[k : k + 1, :].astype(F32) * CAP + position
        meta[0, TOPK + k : TOPK + k + 1, :] = gates_ref[k : k + 1, :]
    meta[0, 2 * TOPK :, :] = jnp.zeros((meta.shape[1] - 2 * TOPK, row_count), F32)
    def swap_copy(i, src, dst):
        return pltpu.make_async_remote_copy(
            src_ref=src, dst_ref=dst, send_sem=swap_sem.at[0, i], recv_sem=swap_sem.at[1, i],
            device_id=far_peer, device_id_type=MESH,
        )

    swaps = [
        swap_copy(0, tok_ref.at[:, cols(1 - x_me, wide)], halves.at[0]),
        swap_copy(1, cot_ref.at[:, cols(1 - x_me, wide)], halves.at[1]),
        swap_copy(2, meta.at[0], meta.at[1]),
    ]
    slot_ids = lax.broadcasted_iota(jnp.int32, (slot_total, row_count), 0).astype(F32)

    def placed(s):
        return [slot_ids == meta[s, k : k + 1, :] for k in range(TOPK)]

    def fill(s, tok, cot):
        picks = placed(s)
        selector = sum(jnp.where(p, 1.0, 0.0) for p in picks).astype(BF16)
        weight = sum(
            jnp.where(p, meta[s, TOPK + k : TOPK + k + 1, :], 0.0) for k, p in enumerate(picks)
        )
        weight = jnp.sum(weight, axis=1, keepdims=True)
        send[s, 0] = jnp.dot(selector, tok, preferred_element_type=F32).astype(BF16)
        send[s, 1] = (jnp.dot(selector, cot, preferred_element_type=F32) * weight).astype(BF16)

    def place(k, j):
        zh = lax.rem(zh_me + j // 2, n_zh)
        z = zh * 2 + lax.rem(zl_me + k % 2, 2)
        e = z * 2 + lax.rem(y_me + k // 2, 2)
        return e, zh, lax.rem(c_me + lax.rem(j, 2), 2)

    def source_dp(s, c):
        return (x_me if s == 0 else 1 - x_me) * 2 + c

    def in_copy(k, s, j):
        e, zh, c = place(k, j)
        pos = zh_me * n_dp + source_dp(s, c_me)
        return pltpu.make_async_remote_copy(
            src_ref=send.at[s, :, band(e), cols(c, width)],
            dst_ref=recv.at[k, pos],
            send_sem=in_send.at[k * per + zh * n_dp + c * 2 + s],
            recv_sem=in_recv.at[k * per + pos],
            device_id=(e, x_me * 2 + c),
            device_id_type=MESH,
        )

    def in_wait(k, s, j):
        e, zh, c = place(k, j)
        pos = zh * n_dp + source_dp(s, c)
        pltpu.make_async_remote_copy(
            src_ref=recv.at[k, pos],
            dst_ref=recv.at[k, pos],
            send_sem=in_send.at[k * per + zh * n_dp + c * 2 + s],
            recv_sem=in_recv.at[k * per + pos],
            device_id=(e, x_me * 2 + c),
            device_id_type=MESH,
        ).wait_recv()

    def out_copy(k, s, j):
        e, zh, c = place(k, j)
        return pltpu.make_async_remote_copy(
            src_ref=ret_send.at[k, zh * n_dp + source_dp(s, c)],
            dst_ref=ret.at[s, :, band(e_me), cols(c_me, width)],
            send_sem=out_send.at[k * per + zh * n_dp + c * 2 + s],
            recv_sem=out_recv.at[k * per + zh_me * n_dp + c_me * 2 + s],
            device_id=(e, x_me * 2 + c),
            device_id_type=MESH,
        )

    def out_wait(k, s, j):
        e, zh, c = place(k, j)
        spot = ret.at[s, :, band(e), cols(c, width)]
        pltpu.make_async_remote_copy(
            src_ref=spot,
            dst_ref=spot,
            send_sem=out_send.at[k * per + zh * n_dp + c * 2 + s],
            recv_sem=out_recv.at[k * per + zh * n_dp + c * 2 + s],
            device_id=(e, x_me * 2 + c),
            device_id_type=MESH,
        ).wait_recv()

    def each(k, body):
        count = n_zh * 2

        def step(j, carry):
            body(j)
            return carry

        lax.fori_loop(1 if k == 0 else 0, count, step, 0)

    def own_in(s):
        return pltpu.make_async_copy(
            send.at[s, :, band(e_me), cols(c_me, width)],
            recv.at[0, zh_me * n_dp + source_dp(s, c_me)],
            local_sem.at[3 + s],
        )

    def own_out(s):
        return pltpu.make_async_copy(
            ret_send.at[0, zh_me * n_dp + source_dp(s, c_me)],
            ret.at[s, :, band(e_me), cols(c_me, width)],
            local_sem.at[3 + s],
        )

    def send_chunk(k, s):
        each(k, lambda j: in_copy(k, s, j).start())
        if k == 0:
            own_in(s).start()

    fill(0, tok_ref[:, cols(x_me, wide)], cot_ref[:, cols(x_me, wide)])
    pl.semaphore_wait(barrier, plane)
    for copy in swaps:
        copy.start()
    send_chunk(0, 0)
    send_chunk(1, 0)
    for copy in swaps:
        copy.wait_recv()
    fill(1, halves[0], halves[1])
    for k, s in ((0, 1), (1, 1), (2, 0), (2, 1), (3, 0), (3, 1)):
        send_chunk(k, s)
    for copy in input_copies[4:]:
        copy.wait()
    for copy in weight_copies:
        copy.wait()

    def pair_copy(k, src, dst, peer, stage):
        i = stage * 4 + k
        return pltpu.make_async_remote_copy(
            src_ref=src, dst_ref=dst, send_sem=pair_sem.at[0, i], recv_sem=pair_sem.at[1, i],
            device_id=peer, device_id_type=MESH,
        )

    def span(k):
        return pl.ds(k * part, part)

    mine = pl.ds(c_me * half, half)
    core_copy = [pair_copy(k, psend.at[k], crecv.at[k], core_peer, 0) for k in range(4)]
    far_copy = [pair_copy(k, xsend.at[k], xrecv.at[k], far_peer, 1) for k in range(4)]
    hid_copy = [
        pair_copy(k, hid.at[mine, span(k)], hid.at[mine, span(k)], core_peer, 2) for k in range(4)
    ]

    def partial(k, e, col):
        if col == 2:
            return jnp.dot(rows[e, span(k), width:], wd[e], preferred_element_type=F32)
        return jnp.dot(rows[e, span(k), :width], (wg, wu)[col][e], preferred_element_type=F32)

    def first_stage(k):
        for s in range(2):
            if k == 0:
                own_in(s).wait()
            each(k, lambda j, s=s: in_wait(k, s, j))
        for t in range(2):
            block = recv[k, :, t].reshape(per * msg, width)
            moved = jnp.dot(perm_ref[...], block, preferred_element_type=F32).astype(BF16)
            rows[:, k * part : (k + 1) * part, t * width : (t + 1) * width] = moved.reshape(
                el, part, width
            )

        def other(j, carry):
            for col in range(3):
                psend[k, j, :, col * ff : (col + 1) * ff] = partial(
                    k, (1 - c_me) * half + j, col
                ).astype(BF16)
            return carry

        lax.fori_loop(0, half, other, 0, unroll=True)
        core_copy[k].start()

        def own(j, carry):
            for col in range(3):
                pown[k, j, :, col * ff : (col + 1) * ff] = partial(k, c_me * half + j, col)
            return carry

        lax.fori_loop(0, half, own, 0, unroll=True)

    def chip_sum(k):
        core_copy[k].wait_recv()

        def body(j, carry):
            s = pown[k, j] + crecv[k, j].astype(F32)
            pown[k, j] = s
            xsend[k, j] = s.astype(BF16)
            return carry

        lax.fori_loop(0, half, body, 0)
        far_copy[k].start()

    def middle(k):
        far_copy[k].wait_recv()

        def body(j, carry):
            s = pown[k, j] + xrecv[k, j].astype(F32)
            gate_pre, up_pre, hidden_grad = s[:, :ff], s[:, ff : 2 * ff], s[:, 2 * ff :]
            sig = jax.nn.sigmoid(gate_pre)
            act = gate_pre * sig
            e = c_me * half + j
            hid[e, span(k), :ff] = (act * up_pre).astype(BF16)
            hid[e, span(k), ff : 2 * ff] = (
                hidden_grad * up_pre * sig * (1.0 + gate_pre * (1.0 - sig))
            ).astype(BF16)
            hid[e, span(k), 2 * ff :] = (hidden_grad * act).astype(BF16)
            return carry

        lax.fori_loop(0, half, body, 0)
        hid_copy[k].start()

    last = (((1,), (1,)), ((), ()))
    first = (((0,), (0,)), ((), ()))

    def last_stage(k):
        def body(j, carry, base):
            e = base + j
            h = hid[e, span(k)]
            pre_ret[0, e] = lax.dot_general(
                h[:, :ff], wd[e], last, preferred_element_type=F32
            ).astype(BF16)
            pre_ret[1, e] = (
                lax.dot_general(h[:, ff : 2 * ff], wg[e], last, preferred_element_type=F32)
                + lax.dot_general(h[:, 2 * ff :], wu[e], last, preferred_element_type=F32)
            ).astype(BF16)
            return carry

        lax.fori_loop(0, half, functools.partial(body, base=c_me * half), 0, unroll=True)
        hid_copy[k].wait_recv()
        lax.fori_loop(0, half, functools.partial(body, base=(1 - c_me) * half), 0, unroll=True)
        for t in range(2):
            block = pre_ret[t].reshape(el * part, width)
            moved = jnp.dot(back_ref[...], block, preferred_element_type=F32).astype(BF16)
            ret_send[k, :, t] = moved.reshape(per, msg, width)
        for s in (1, 0):
            each(k, lambda j, s=s: out_copy(k, s, j).start())
            if k == 0:
                own_out(s).start()

    first_stage(0)
    chip_sum(0)
    first_stage(1)
    chip_sum(1)
    first_stage(2)
    chip_sum(2)
    middle(0)
    last_stage(0)
    first_stage(3)
    chip_sum(3)
    for k in range(1, 4):
        middle(k)
        last_stage(k)

    def grads(e, carry):
        tok, grad = rows[e, :, :width], rows[e, :, width:]
        h = hid[e]
        dg[e] = lax.dot_general(tok, h[:, ff : 2 * ff], first, preferred_element_type=F32)
        du[e] = lax.dot_general(tok, h[:, 2 * ff :], first, preferred_element_type=F32)
        dd[e] = lax.dot_general(grad, h[:, :ff], first, preferred_element_type=F32)
        return carry

    lax.fori_loop(0, half, grads, 0)

    def combine(s):
        picks = [jnp.where(p, 1.0, 0.0) for p in placed(s)]
        out = 0.0
        for k in range(TOPK):
            gate = jnp.sum(
                jnp.where(row_ids == col_ids, meta[s, TOPK + k : TOPK + k + 1, :], 0.0),
                axis=1,
                keepdims=True,
            )
            picked = lax.dot_general(
                picks[k].astype(BF16), ret[s, 0], first, preferred_element_type=F32
            )
            out = out + gate * picked
        grad = lax.dot_general(
            sum(picks).astype(BF16), ret[s, 1], first, preferred_element_type=F32
        )
        return out.astype(BF16), grad.astype(BF16)

    fin_copy = [swap_copy(3 + i, fin_send.at[i], fin_recv.at[i]) for i in range(2)]
    for s in (1, 0):
        own_out(s).wait()
        for k in range(4):
            each(k, lambda j, k=k, s=s: out_wait(k, s, j))
        out, grad = combine(s)
        if s == 1:
            fin_send[0] = out
            fin_send[1] = grad
            for copy in fin_copy:
                copy.start()
            lax.fori_loop(half, el, grads, 0)
        else:
            layer_ref[:, cols(x_me, wide)] = out
            igrad_ref[:, cols(x_me, wide)] = grad
    for copy in swaps:
        copy.wait_send()
    for k in range(4):
        for s in range(2):
            each(k, lambda j, k=k, s=s: in_copy(k, s, j).wait_send())
            each(k, lambda j, k=k, s=s: out_copy(k, s, j).wait_send())
        core_copy[k].wait_send()
        far_copy[k].wait_send()
        hid_copy[k].wait_send()

    for copy in fin_copy:
        copy.wait()
    layer_ref[:, cols(1 - x_me, wide)] = fin_recv[0]
    igrad_ref[:, cols(1 - x_me, wide)] = fin_recv[1]


def store_kernel(layer, igrad, dg, du, dd, layer_out, igrad_out, dg_out, du_out, dd_out, sem):
    pairs = [
        (src.at[e], dst.at[e])
        for e in range(dg.shape[0])
        for src, dst in ((dg, dg_out), (du, du_out), (dd, dd_out))
    ]
    pairs += [(layer, layer_out), (igrad, igrad_out)]
    copies = [pltpu.make_async_copy(src, dst, sem.at[i]) for i, (src, dst) in enumerate(pairs)]
    for copy in copies:
        copy.start()
    for copy in copies:
        copy.wait()


def shards(tokens, routes, gate_values, cotangent, gating_weight, upward_weight, down_weight):
    n_expert, n_dp = lax.axis_size("expert"), lax.axis_size("dp")
    el, width, ff = gating_weight.shape
    row_count = tokens.shape[0]
    per = n_expert * n_dp // 4
    msg = el * CAP
    part = per * CAP
    slots = 4 * part
    half = el // 2
    wide = 3 * ff
    spot = np.arange(per * msg)
    e, s, c = spot // part, spot % part // CAP, spot % CAP
    perm = np.zeros((per * msg, per * msg), np.float32)
    perm[spot, s * msg + e * CAP + c] = 1.0
    hbm = pl.BlockSpec(memory_space=pltpu.HBM)
    vmem = pl.BlockSpec(memory_space=pltpu.VMEM)
    weight_shape = gating_weight.shape
    layer_output, input_grad, dg, du, dd = pl.pallas_call(
        functools.partial(plane_kernel, n_expert, n_dp, el, width),
        out_shape=(
            pltpu.VMEM(tokens.shape, BF16),
            pltpu.VMEM(tokens.shape, BF16),
            pltpu.VMEM(weight_shape, F32),
            pltpu.VMEM(weight_shape, F32),
            pltpu.VMEM(weight_shape, F32),
        ),
        in_specs=[hbm] * 9,
        out_specs=[vmem] * 5,
        scratch_shapes=[
            pltpu.VMEM(tokens.shape, BF16),
            pltpu.VMEM(tokens.shape, BF16),
            pltpu.VMEM((TOPK, row_count), jnp.int32),
            pltpu.VMEM((TOPK, row_count), F32),
            pltpu.VMEM(perm.shape, BF16),
            pltpu.VMEM(perm.shape, BF16),
            pltpu.VMEM(weight_shape, BF16),
            pltpu.VMEM(weight_shape, BF16),
            pltpu.VMEM(weight_shape, BF16),
            pltpu.VMEM((2, row_count, 2 * width), BF16),
            pltpu.VMEM((2, 8, row_count), F32),
            pltpu.VMEM((2, 2, n_expert * msg, 2 * width), BF16),
            pltpu.VMEM((4, per, 2, msg, width), BF16),
            pltpu.VMEM((el, slots, 2 * width), BF16),
            pltpu.VMEM((4, half, part, wide), BF16),
            pltpu.VMEM((4, half, part, wide), F32),
            pltpu.VMEM((4, half, part, wide), BF16),
            pltpu.VMEM((4, half, part, wide), BF16),
            pltpu.VMEM((4, half, part, wide), BF16),
            pltpu.VMEM((el, slots, wide), BF16),
            pltpu.VMEM((2, el, part, width), BF16),
            pltpu.VMEM((4, per, 2, msg, width), BF16),
            pltpu.VMEM((2, 2, n_expert * msg, 2 * width), BF16),
            pltpu.VMEM((2, row_count, 2 * width), BF16),
            pltpu.VMEM((2, row_count, 2 * width), BF16),
            pltpu.SemaphoreType.DMA((4 * per,)),
            pltpu.SemaphoreType.DMA((4 * per,)),
            pltpu.SemaphoreType.DMA((4 * per,)),
            pltpu.SemaphoreType.DMA((4 * per,)),
            pltpu.SemaphoreType.DMA((2, 12)),
            pltpu.SemaphoreType.DMA((2, 5)),
            pltpu.SemaphoreType.DMA((11,)),
        ],
        compiler_params=pltpu.CompilerParams(
            collective_id=0, has_side_effects=True, vmem_limit_bytes=44 * 1024 * 1024
        ),
    )(
        *(
            pltpu.with_memory_space_constraint(a, pltpu.HBM)
            for a in (
                tokens,
                cotangent,
                routes.T,
                gate_values.T,
                jnp.asarray(perm, BF16),
                jnp.asarray(perm.T, BF16),
                gating_weight,
                upward_weight,
                down_weight,
            )
        )
    )
    results = (layer_output, input_grad, dg, du, dd)
    return pl.pallas_call(
        store_kernel,
        out_shape=tuple(jax.ShapeDtypeStruct(r.shape, r.dtype) for r in results),
        in_specs=[vmem] * 5,
        out_specs=[hbm] * 5,
        scratch_shapes=[pltpu.SemaphoreType.DMA((2 + 3 * el,))],
        compiler_params=pltpu.CompilerParams(vmem_limit_bytes=16 * 1024 * 1024),
    )(*results)


def general_shards(tokens, routes, gate_values, cotangent, gating_weight, upward_weight, down_weight):
    expert_total = gating_weight.shape[0] * lax.axis_size("expert")
    row_count = tokens.shape[0]
    slot_total = expert_total * CAP
    flat_routes = routes.reshape(-1)
    onehot = (flat_routes[:, None] == jnp.arange(expert_total, dtype=jnp.int32)[None, :]).astype(
        jnp.int32
    )
    position = jnp.sum((jnp.cumsum(onehot, axis=0) - onehot) * onehot, axis=1)
    slot_index = flat_routes * CAP + position
    placed = (slot_index[:, None] == jnp.arange(slot_total, dtype=jnp.int32)[None, :]).astype(
        jnp.float32
    )
    placed = placed.reshape(row_count, TOPK, slot_total)
    selector = jnp.sum(placed, axis=1).astype(jnp.bfloat16)
    slot_gate = jnp.sum(placed * gate_values[:, :, None], axis=(0, 1))
    contract = (((0,), (0,)), ((), ()))
    send_rows = lax.dot_general(selector, tokens, contract, preferred_element_type=jnp.float32)
    send_rows = send_rows.astype(jnp.bfloat16).reshape(expert_total, CAP, -1)
    slot_cotangent = lax.dot_general(
        selector, cotangent, contract, preferred_element_type=jnp.float32
    )
    send_grads = (
        (slot_cotangent * slot_gate[:, None]).astype(jnp.bfloat16).reshape(expert_total, CAP, -1)
    )
    arrived, arrived_grad = (
        lax.all_to_all(send_rows, "expert", split_axis=0, concat_axis=1, tiled=True),
        lax.all_to_all(send_grads, "expert", split_axis=0, concat_axis=1, tiled=True),
    )
    gating, upward, lowering = (
        lax.all_gather(gating_weight, "dp", axis=1, tiled=True),
        lax.all_gather(upward_weight, "dp", axis=1, tiled=True),
        lax.all_gather(down_weight, "dp", axis=1, tiled=True),
    )
    gate_pre = jnp.einsum("erd,edf->erf", arrived, gating, preferred_element_type=jnp.float32)
    up_pre = jnp.einsum("erd,edf->erf", arrived, upward, preferred_element_type=jnp.float32)
    sigmoid_gate = jax.nn.sigmoid(gate_pre)
    activated = gate_pre * sigmoid_gate
    hidden = (activated * up_pre).astype(jnp.bfloat16)
    expert_out = jnp.einsum(
        "erf,edf->erd", hidden, lowering, preferred_element_type=jnp.float32
    ).astype(jnp.bfloat16)
    gating, upward, lowering = (
        lax.all_gather(gating_weight, "dp", axis=1, tiled=True),
        lax.all_gather(upward_weight, "dp", axis=1, tiled=True),
        lax.all_gather(down_weight, "dp", axis=1, tiled=True),
    )
    hidden_grad = jnp.einsum(
        "erd,edf->erf", arrived_grad, lowering, preferred_element_type=jnp.float32
    )
    gate_part = (
        hidden_grad * up_pre * sigmoid_gate * (1.0 + gate_pre * (1.0 - sigmoid_gate))
    ).astype(jnp.bfloat16)
    up_part = (hidden_grad * activated).astype(jnp.bfloat16)
    pair_grad = (
        jnp.einsum("erf,edf->erd", gate_part, gating, preferred_element_type=jnp.float32)
        + jnp.einsum("erf,edf->erd", up_part, upward, preferred_element_type=jnp.float32)
    ).astype(jnp.bfloat16)
    returned_out, returned_grad = (
        lax.all_to_all(expert_out, "expert", split_axis=1, concat_axis=0, tiled=True),
        lax.all_to_all(pair_grad, "expert", split_axis=1, concat_axis=0, tiled=True),
    )
    gating_term = jnp.einsum("erd,erf->edf", arrived, gate_part, preferred_element_type=jnp.float32)
    upward_term = jnp.einsum("erd,erf->edf", arrived, up_part, preferred_element_type=jnp.float32)
    down_term = jnp.einsum("erd,erf->edf", arrived_grad, hidden, preferred_element_type=jnp.float32)
    gating_grad, upward_grad, down_grad = (
        lax.psum_scatter(
            gating_term.astype(jnp.bfloat16), "dp", scatter_dimension=1, tiled=True
        ).astype(jnp.float32),
        lax.psum_scatter(
            upward_term.astype(jnp.bfloat16), "dp", scatter_dimension=1, tiled=True
        ).astype(jnp.float32),
        lax.psum_scatter(
            down_term.astype(jnp.bfloat16), "dp", scatter_dimension=1, tiled=True
        ).astype(jnp.float32),
    )
    returned_flat = returned_out.reshape(slot_total, -1)
    combined = jnp.zeros((row_count, returned_flat.shape[1]), jnp.float32)
    for choice_slot in range(TOPK):
        picker = placed[:, choice_slot, :].astype(jnp.bfloat16)
        picked = jnp.dot(picker, returned_flat, preferred_element_type=jnp.float32)
        combined = combined + gate_values[:, choice_slot][:, None] * picked
    layer_output = combined.astype(jnp.bfloat16)
    input_grad = jnp.dot(
        selector, returned_grad.reshape(slot_total, -1), preferred_element_type=jnp.float32
    ).astype(jnp.bfloat16)
    return (layer_output, input_grad, gating_grad, upward_grad, down_grad)


def solution(mesh):
    n_expert, n_dp = mesh.shape["expert"], mesh.shape["dp"]

    def program(*args):
        el = args[4].shape[0] // n_expert
        width = args[4].shape[1] // n_dp
        part = n_expert * n_dp // 4 * CAP
        fits = (
            n_dp == 4
            and n_expert % 4 == 0
            and el % 2 == 0
            and el * CAP % 16 == 0
            and part % 16 == 0
            and width % 128 == 0
            and args[4].shape[2] % 128 == 0
            and args[0].shape[0] // (n_expert * n_dp) % 128 == 0
        )
        return jax.shard_map(
            shards if fits else general_shards,
            mesh=mesh,
            in_specs=(
                P(("expert", "dp"), None),
                P(("expert", "dp"), None),
                P(("expert", "dp"), None),
                P(("expert", "dp"), None),
                P("expert", "dp", None),
                P("expert", "dp", None),
                P("expert", "dp", None),
            ),
            out_specs=(
                P(("expert", "dp"), None),
                P(("expert", "dp"), None),
                P("expert", "dp", None),
                P("expert", "dp", None),
                P("expert", "dp", None),
            ),
            check_vma=False,
        )(*args)

    return program
```

```python
import functools
import jax
import jax.numpy as jnp
import numpy as np
from jax import lax
from jax.experimental import pallas as pl
from jax.experimental.pallas import tpu as pltpu
from jax.sharding import PartitionSpec as P

TOPK = 2
CAP = 6
MESH = pl.DeviceIdType.MESH
F32 = jnp.float32
BF16 = jnp.bfloat16
GROUPS = (((0, 0, 0), (1, 0, 0)), ((0, 1, 0), (1, 1, 0)), ((0, 0, 1), (1, 0, 1)), ((0, 1, 1), (1, 1, 1)))
RETURNS = (((0, 1, 1), (0, 0, 1), (0, 1, 0), (0, 0, 0)), ((1, 1, 1), (1, 0, 1), (1, 1, 0), (1, 0, 0)), ((2, 1, 1), (2, 0, 1), (2, 1, 0), (2, 0, 0)), ((3, 1, 1), (3, 0, 1), (3, 1, 0), (3, 0, 0)))
STEPS = (('send', ((0, 0, 0), (0, 1, 0), (1, 0, 0), (1, 1, 0))), ('load', 0), ('swap', 0), ('send', ((0, 0, 1), (0, 1, 1), (1, 0, 1), (1, 1, 1))), ('rows', 0), ('chip', 0), ('send', ((2, 0, 0), (2, 1, 0), (2, 0, 1), (2, 1, 1))), ('rows', 1), ('send', ((3, 0, 0), (3, 1, 0), (3, 0, 1), (3, 1, 1))), ('chip', 1), ('act', 0), ('rows', 2), ('chip', 2), ('act', 1), ('rows', 3), ('chip', 3), ('act', 2), ('act', 3))


def plane_kernel(
    n_expert, n_dp, el, width,
    tok_in, cot_in, routes_in, gates_in, perm_in, back_in, wg_ref, wu_ref, wd_ref,
    layer_ref, igrad_ref, dg, du, dd,
    tok_ref, cot_ref, routes_ref, gates_ref, perm_ref, back_ref,
    wg, wu, wd, halves, meta, send, recv, rows, psend, pown, crecv, xsend, xrecv, hid,
    pre_ret, ret_send, ret, fin_send, fin_recv,
    in_send, in_recv, out_send, out_recv, pair_sem, swap_sem, local_sem,
):
    e_me = lax.axis_index("expert")
    d_me = lax.axis_index("dp")
    z_me, y_me = e_me // 2, lax.rem(e_me, 2)
    zh_me, zl_me = z_me // 2, lax.rem(z_me, 2)
    x_me, c_me = d_me // 2, lax.rem(d_me, 2)
    core_peer = (e_me, x_me * 2 + 1 - c_me)
    far_peer = (e_me, (1 - x_me) * 2 + c_me)
    per = n_dp * len(GROUPS[0])
    msg = el * CAP
    part = per * CAP
    half = el // 2
    ff = wg.shape[2]
    row_count = tok_ref.shape[0]
    slot_total = n_expert * msg
    wide = 2 * width
    plane = n_expert * 2

    def cols(index, size):
        return pl.ds(pl.multiple_of(index * size, size), size)

    def band(e):
        return pl.ds(pl.multiple_of(e * msg, msg), msg)

    input_copies = [
        pltpu.make_async_copy(src, dst, local_sem.at[5 + i])
        for i, (src, dst) in enumerate(
            (
                (routes_in, routes_ref), (gates_in, gates_ref), (tok_in, tok_ref), (cot_in, cot_ref),
                (perm_in, perm_ref), (back_in, back_ref),
            )
        )
    ]
    barrier = pltpu.get_barrier_semaphore()

    def greet(off, carry):
        other = lax.rem(e_me * 2 + c_me + off, plane)
        pl.semaphore_signal(
            barrier, inc=1, device_id=(other // 2, x_me * 2 + lax.rem(other, 2)), device_id_type=MESH
        )
        return carry

    lax.fori_loop(1, plane, greet, 0)
    pl.semaphore_signal(barrier, inc=1, device_id=far_peer, device_id_type=MESH)
    weight_copies = [
        pltpu.make_async_copy(src, dst, local_sem.at[i])
        for i, (src, dst) in enumerate(((wg_ref, wg), (wu_ref, wu), (wd_ref, wd)))
    ]
    for copy in input_copies:
        copy.start()
    for copy in weight_copies:
        copy.start()
    for copy in input_copies[:4]:
        copy.wait()

    expert_ids = lax.broadcasted_iota(jnp.int32, (n_expert * el, row_count), 0)
    named = [expert_ids == routes_ref[k : k + 1, :] for k in range(TOPK)]
    either = sum(jnp.where(n, 1.0, 0.0) for n in named).astype(BF16)
    square = (row_count, row_count)
    row_ids, col_ids = lax.broadcasted_iota(jnp.int32, square, 0), lax.broadcasted_iota(jnp.int32, square, 1)
    earlier = jnp.where(row_ids < col_ids, 1.0, 0.0).astype(BF16)
    before = jnp.dot(either, earlier, preferred_element_type=F32)
    for k in range(TOPK):
        position = jnp.sum(jnp.where(named[k], before, 0.0), axis=0, keepdims=True)
        meta[0, k : k + 1, :] = routes_ref[k : k + 1, :].astype(F32) * CAP + position
        meta[0, TOPK + k : TOPK + k + 1, :] = gates_ref[k : k + 1, :]
    meta[0, 2 * TOPK :, :] = jnp.zeros((meta.shape[1] - 2 * TOPK, row_count), F32)
    def swap_copy(i, src, dst):
        return pltpu.make_async_remote_copy(
            src_ref=src, dst_ref=dst, send_sem=swap_sem.at[0, i], recv_sem=swap_sem.at[1, i],
            device_id=far_peer, device_id_type=MESH,
        )

    swaps = [
        swap_copy(0, tok_ref.at[:, cols(1 - x_me, wide)], halves.at[0]),
        swap_copy(1, cot_ref.at[:, cols(1 - x_me, wide)], halves.at[1]),
        swap_copy(2, meta.at[0], meta.at[1]),
    ]
    slot_ids = lax.broadcasted_iota(jnp.int32, (slot_total, row_count), 0).astype(F32)

    def placed(s):
        return [slot_ids == meta[s, k : k + 1, :] for k in range(TOPK)]

    def fill(s, tok, cot):
        picks = placed(s)
        selector = sum(jnp.where(p, 1.0, 0.0) for p in picks).astype(BF16)
        weight = sum(
            jnp.where(p, meta[s, TOPK + k : TOPK + k + 1, :], 0.0) for k, p in enumerate(picks)
        )
        weight = jnp.sum(weight, axis=1, keepdims=True)
        send[s, 0] = jnp.dot(selector, tok, preferred_element_type=F32).astype(BF16)
        send[s, 1] = (jnp.dot(selector, cot, preferred_element_type=F32) * weight).astype(BF16)

    def place(g, i, j):
        far, zl, y = GROUPS[g][i]
        z = lax.rem(zh_me + far, 2) * 2 + lax.rem(zl_me + zl, 2)
        return z * 2 + lax.rem(y_me + y, 2), lax.rem(c_me + j, 2)

    def home(g, i, j):
        return not any(GROUPS[g][i]) and j == 0

    def spot(i, s, c):
        return i * n_dp + (x_me if s == 0 else 1 - x_me) * 2 + c

    def message(g, i, s, j, src, dst, sems):
        e, c = place(g, i, j)
        return pltpu.make_async_remote_copy(
            src_ref=src,
            dst_ref=dst,
            send_sem=sems[0].at[g * per + spot(i, s, c)],
            recv_sem=sems[1].at[g * per + spot(i, s, c_me)],
            device_id=(e, x_me * 2 + c),
            device_id_type=MESH,
        )

    def in_copy(g, i, s, j):
        e, c = place(g, i, j)
        src = send.at[s, :, band(e), cols(c, width)]
        dst = recv.at[g, spot(i, s, c_me)]
        if home(g, i, j):
            return pltpu.make_async_copy(src, dst, local_sem.at[3 + s])
        return message(g, i, s, j, src, dst, (in_send, in_recv))

    def out_copy(g, i, s, j):
        e, c = place(g, i, j)
        src = ret_send.at[g, spot(i, s, c)]
        dst = ret.at[s, :, band(e_me), cols(c_me, width)]
        if home(g, i, j):
            return pltpu.make_async_copy(src, dst, local_sem.at[3 + s])
        return message(g, i, s, j, src, dst, (out_send, out_recv))

    def arrival(g, i, s, j, place_in, sems):
        e, c = place(g, i, j)
        return pltpu.make_async_remote_copy(
            src_ref=place_in,
            dst_ref=place_in,
            send_sem=sems[0].at[g * per + spot(i, s, c)],
            recv_sem=sems[1].at[g * per + spot(i, s, c)],
            device_id=(e, x_me * 2 + c),
            device_id_type=MESH,
        )

    def in_wait(g, i, s):
        for j in range(2):
            if home(g, i, j):
                in_copy(g, i, s, j).wait()
            else:
                c = place(g, i, j)[1]
                arrival(g, i, s, j, recv.at[g, spot(i, s, c)], (in_send, in_recv)).wait_recv()

    def out_wait(g, i, s):
        for j in range(2):
            if home(g, i, j):
                out_copy(g, i, s, j).wait()
            else:
                e, c = place(g, i, j)
                landed = ret.at[s, :, band(e), cols(c, width)]
                arrival(g, i, s, j, landed, (out_send, out_recv)).wait_recv()

    members = [(g, i) for g, group in enumerate(GROUPS) for i in range(len(group))]

    def send_out(messages):
        for g, i, s in messages:
            for j in (1, 0):
                in_copy(g, i, s, j).start()

    fill(0, tok_ref[:, cols(x_me, wide)], cot_ref[:, cols(x_me, wide)])
    pl.semaphore_wait(barrier, plane)
    for copy in swaps:
        copy.start()

    def pair_copy(k, src, dst, peer, stage):
        i = stage * 4 + k
        return pltpu.make_async_remote_copy(
            src_ref=src, dst_ref=dst, send_sem=pair_sem.at[0, i], recv_sem=pair_sem.at[1, i],
            device_id=peer, device_id_type=MESH,
        )

    def span(k):
        return pl.ds(k * part, part)

    mine = pl.ds(c_me * half, half)
    core_copy = [pair_copy(k, psend.at[k], crecv.at[k], core_peer, 0) for k in range(4)]
    far_copy = [pair_copy(k, xsend.at[k], xrecv.at[k], far_peer, 1) for k in range(4)]
    hid_copy = [
        pair_copy(k, hid.at[mine, span(k)], hid.at[mine, span(k)], core_peer, 2) for k in range(4)
    ]

    def partial(k, e, col):
        if col == 2:
            return jnp.dot(rows[e, span(k), width:], wd[e], preferred_element_type=F32)
        return jnp.dot(rows[e, span(k), :width], (wg, wu)[col][e], preferred_element_type=F32)

    def first_stage(k):
        for s in range(2):
            for i in range(len(GROUPS[k])):
                in_wait(k, i, s)
        for t in range(2):
            block = recv[k, :, t].reshape(per * msg, width)
            moved = jnp.dot(perm_ref[...], block, preferred_element_type=F32).astype(BF16)
            rows[:, k * part : (k + 1) * part, t * width : (t + 1) * width] = moved.reshape(
                el, part, width
            )

        def other(j, carry):
            for col in range(3):
                psend[k, j, :, col * ff : (col + 1) * ff] = partial(
                    k, (1 - c_me) * half + j, col
                ).astype(BF16)
            return carry

        lax.fori_loop(0, half, other, 0, unroll=True)
        core_copy[k].start()

        def own(j, carry):
            for col in range(3):
                pown[k, j, :, col * ff : (col + 1) * ff] = partial(k, c_me * half + j, col)
            return carry

        lax.fori_loop(0, half, own, 0, unroll=True)

    def chip_sum(k):
        core_copy[k].wait_recv()

        def body(j, carry):
            s = pown[k, j] + crecv[k, j].astype(F32)
            pown[k, j] = s
            xsend[k, j] = s.astype(BF16)
            return carry

        lax.fori_loop(0, half, body, 0)
        far_copy[k].start()

    def middle(k):
        far_copy[k].wait_recv()

        def body(j, carry):
            s = pown[k, j] + xrecv[k, j].astype(F32)
            gate_pre, up_pre, hidden_grad = s[:, :ff], s[:, ff : 2 * ff], s[:, 2 * ff :]
            sig = jax.nn.sigmoid(gate_pre)
            act = gate_pre * sig
            e = c_me * half + j
            hid[e, span(k), :ff] = (act * up_pre).astype(BF16)
            hid[e, span(k), ff : 2 * ff] = (
                hidden_grad * up_pre * sig * (1.0 + gate_pre * (1.0 - sig))
            ).astype(BF16)
            hid[e, span(k), 2 * ff :] = (hidden_grad * act).astype(BF16)
            return carry

        lax.fori_loop(0, half, body, 0)
        hid_copy[k].start()

    last = (((1,), (1,)), ((), ()))
    first = (((0,), (0,)), ((), ()))

    def last_stage(k):
        def body(j, carry, base):
            e = base + j
            h = hid[e, span(k)]
            pre_ret[0, e] = lax.dot_general(
                h[:, :ff], wd[e], last, preferred_element_type=F32
            ).astype(BF16)
            pre_ret[1, e] = (
                lax.dot_general(h[:, ff : 2 * ff], wg[e], last, preferred_element_type=F32)
                + lax.dot_general(h[:, 2 * ff :], wu[e], last, preferred_element_type=F32)
            ).astype(BF16)
            return carry

        lax.fori_loop(0, half, functools.partial(body, base=c_me * half), 0, unroll=True)
        hid_copy[k].wait_recv()
        lax.fori_loop(0, half, functools.partial(body, base=(1 - c_me) * half), 0, unroll=True)
        for t in range(2):
            block = pre_ret[t].reshape(el * part, width)
            moved = jnp.dot(back_ref[...], block, preferred_element_type=F32).astype(BF16)
            ret_send[k, :, t] = moved.reshape(per, msg, width)
        for g, i, s in RETURNS[k]:
            for j in (1, 0):
                out_copy(g, i, s, j).start()

    def load(_):
        for copy in input_copies[4:]:
            copy.wait()
        for copy in weight_copies:
            copy.wait()

    def swap_in(_):
        for copy in swaps:
            copy.wait_recv()
        fill(1, halves[0], halves[1])

    def act(k):
        middle(k)
        last_stage(k)

    work = dict(send=send_out, load=load, rows=first_stage, swap=swap_in, chip=chip_sum, act=act)
    for step, k in STEPS:
        work[step](k)

    def grads(e, carry):
        tok, grad = rows[e, :, :width], rows[e, :, width:]
        h = hid[e]
        dg[e] = lax.dot_general(tok, h[:, ff : 2 * ff], first, preferred_element_type=F32)
        du[e] = lax.dot_general(tok, h[:, 2 * ff :], first, preferred_element_type=F32)
        dd[e] = lax.dot_general(grad, h[:, :ff], first, preferred_element_type=F32)
        return carry

    lax.fori_loop(0, half, grads, 0)

    def combine(s):
        picks = [jnp.where(p, 1.0, 0.0) for p in placed(s)]
        out = 0.0
        for k in range(TOPK):
            gate = jnp.sum(
                jnp.where(row_ids == col_ids, meta[s, TOPK + k : TOPK + k + 1, :], 0.0),
                axis=1,
                keepdims=True,
            )
            picked = lax.dot_general(
                picks[k].astype(BF16), ret[s, 0], first, preferred_element_type=F32
            )
            out = out + gate * picked
        grad = lax.dot_general(
            sum(picks).astype(BF16), ret[s, 1], first, preferred_element_type=F32
        )
        return out.astype(BF16), grad.astype(BF16)

    fin_copy = [swap_copy(3 + i, fin_send.at[i], fin_recv.at[i]) for i in range(2)]
    for s in (1, 0):
        for g, i in members:
            out_wait(g, i, s)
        out, grad = combine(s)
        if s == 1:
            fin_send[0] = out
            fin_send[1] = grad
            for copy in fin_copy:
                copy.start()
            lax.fori_loop(half, el, grads, 0)
        else:
            layer_ref[:, cols(x_me, wide)] = out
            igrad_ref[:, cols(x_me, wide)] = grad
    for copy in swaps:
        copy.wait_send()
    for k in range(4):
        for i in range(len(GROUPS[k])):
            for s in range(2):
                for j in range(2):
                    if not home(k, i, j):
                        in_copy(k, i, s, j).wait_send()
                        out_copy(k, i, s, j).wait_send()
        core_copy[k].wait_send()
        far_copy[k].wait_send()
        hid_copy[k].wait_send()

    for copy in fin_copy:
        copy.wait()
    layer_ref[:, cols(1 - x_me, wide)] = fin_recv[0]
    igrad_ref[:, cols(1 - x_me, wide)] = fin_recv[1]


def store_kernel(layer, igrad, dg, du, dd, layer_out, igrad_out, dg_out, du_out, dd_out, sem):
    pairs = [
        (src.at[e], dst.at[e])
        for e in range(dg.shape[0])
        for src, dst in ((dg, dg_out), (du, du_out), (dd, dd_out))
    ]
    pairs += [(layer, layer_out), (igrad, igrad_out)]
    copies = [pltpu.make_async_copy(src, dst, sem.at[i]) for i, (src, dst) in enumerate(pairs)]
    for copy in copies:
        copy.start()
    for copy in copies:
        copy.wait()


def shards(tokens, routes, gate_values, cotangent, gating_weight, upward_weight, down_weight):
    n_expert, n_dp = lax.axis_size("expert"), lax.axis_size("dp")
    el, width, ff = gating_weight.shape
    row_count = tokens.shape[0]
    per = n_expert * n_dp // 4
    msg = el * CAP
    part = per * CAP
    slots = 4 * part
    half = el // 2
    wide = 3 * ff
    spot = np.arange(per * msg)
    e, s, c = spot // part, spot % part // CAP, spot % CAP
    perm = np.zeros((per * msg, per * msg), np.float32)
    perm[spot, s * msg + e * CAP + c] = 1.0
    hbm = pl.BlockSpec(memory_space=pltpu.HBM)
    vmem = pl.BlockSpec(memory_space=pltpu.VMEM)
    weight_shape = gating_weight.shape
    layer_output, input_grad, dg, du, dd = pl.pallas_call(
        functools.partial(plane_kernel, n_expert, n_dp, el, width),
        out_shape=(
            pltpu.VMEM(tokens.shape, BF16),
            pltpu.VMEM(tokens.shape, BF16),
            pltpu.VMEM(weight_shape, F32),
            pltpu.VMEM(weight_shape, F32),
            pltpu.VMEM(weight_shape, F32),
        ),
        in_specs=[hbm] * 9,
        out_specs=[vmem] * 5,
        scratch_shapes=[
            pltpu.VMEM(tokens.shape, BF16),
            pltpu.VMEM(tokens.shape, BF16),
            pltpu.VMEM((TOPK, row_count), jnp.int32),
            pltpu.VMEM((TOPK, row_count), F32),
            pltpu.VMEM(perm.shape, BF16),
            pltpu.VMEM(perm.shape, BF16),
            pltpu.VMEM(weight_shape, BF16),
            pltpu.VMEM(weight_shape, BF16),
            pltpu.VMEM(weight_shape, BF16),
            pltpu.VMEM((2, row_count, 2 * width), BF16),
            pltpu.VMEM((2, 8, row_count), F32),
            pltpu.VMEM((2, 2, n_expert * msg, 2 * width), BF16),
            pltpu.VMEM((4, per, 2, msg, width), BF16),
            pltpu.VMEM((el, slots, 2 * width), BF16),
            pltpu.VMEM((4, half, part, wide), BF16),
            pltpu.VMEM((4, half, part, wide), F32),
            pltpu.VMEM((4, half, part, wide), BF16),
            pltpu.VMEM((4, half, part, wide), BF16),
            pltpu.VMEM((4, half, part, wide), BF16),
            pltpu.VMEM((el, slots, wide), BF16),
            pltpu.VMEM((2, el, part, width), BF16),
            pltpu.VMEM((4, per, 2, msg, width), BF16),
            pltpu.VMEM((2, 2, n_expert * msg, 2 * width), BF16),
            pltpu.VMEM((2, row_count, 2 * width), BF16),
            pltpu.VMEM((2, row_count, 2 * width), BF16),
            pltpu.SemaphoreType.DMA((4 * per,)),
            pltpu.SemaphoreType.DMA((4 * per,)),
            pltpu.SemaphoreType.DMA((4 * per,)),
            pltpu.SemaphoreType.DMA((4 * per,)),
            pltpu.SemaphoreType.DMA((2, 12)),
            pltpu.SemaphoreType.DMA((2, 5)),
            pltpu.SemaphoreType.DMA((11,)),
        ],
        compiler_params=pltpu.CompilerParams(
            collective_id=0, has_side_effects=True, vmem_limit_bytes=44 * 1024 * 1024
        ),
    )(
        *(
            pltpu.with_memory_space_constraint(a, pltpu.HBM)
            for a in (
                tokens,
                cotangent,
                routes.T,
                gate_values.T,
                jnp.asarray(perm, BF16),
                jnp.asarray(perm.T, BF16),
                gating_weight,
                upward_weight,
                down_weight,
            )
        )
    )
    results = (layer_output, input_grad, dg, du, dd)
    return pl.pallas_call(
        store_kernel,
        out_shape=tuple(jax.ShapeDtypeStruct(r.shape, r.dtype) for r in results),
        in_specs=[vmem] * 5,
        out_specs=[hbm] * 5,
        scratch_shapes=[pltpu.SemaphoreType.DMA((2 + 3 * el,))],
        compiler_params=pltpu.CompilerParams(vmem_limit_bytes=16 * 1024 * 1024),
    )(*results)


def general_shards(tokens, routes, gate_values, cotangent, gating_weight, upward_weight, down_weight):
    expert_total = gating_weight.shape[0] * lax.axis_size("expert")
    row_count = tokens.shape[0]
    slot_total = expert_total * CAP
    flat_routes = routes.reshape(-1)
    onehot = (flat_routes[:, None] == jnp.arange(expert_total, dtype=jnp.int32)[None, :]).astype(
        jnp.int32
    )
    position = jnp.sum((jnp.cumsum(onehot, axis=0) - onehot) * onehot, axis=1)
    slot_index = flat_routes * CAP + position
    placed = (slot_index[:, None] == jnp.arange(slot_total, dtype=jnp.int32)[None, :]).astype(
        jnp.float32
    )
    placed = placed.reshape(row_count, TOPK, slot_total)
    selector = jnp.sum(placed, axis=1).astype(jnp.bfloat16)
    slot_gate = jnp.sum(placed * gate_values[:, :, None], axis=(0, 1))
    contract = (((0,), (0,)), ((), ()))
    send_rows = lax.dot_general(selector, tokens, contract, preferred_element_type=jnp.float32)
    send_rows = send_rows.astype(jnp.bfloat16).reshape(expert_total, CAP, -1)
    slot_cotangent = lax.dot_general(
        selector, cotangent, contract, preferred_element_type=jnp.float32
    )
    send_grads = (
        (slot_cotangent * slot_gate[:, None]).astype(jnp.bfloat16).reshape(expert_total, CAP, -1)
    )
    arrived, arrived_grad = (
        lax.all_to_all(send_rows, "expert", split_axis=0, concat_axis=1, tiled=True),
        lax.all_to_all(send_grads, "expert", split_axis=0, concat_axis=1, tiled=True),
    )
    gating, upward, lowering = (
        lax.all_gather(gating_weight, "dp", axis=1, tiled=True),
        lax.all_gather(upward_weight, "dp", axis=1, tiled=True),
        lax.all_gather(down_weight, "dp", axis=1, tiled=True),
    )
    gate_pre = jnp.einsum("erd,edf->erf", arrived, gating, preferred_element_type=jnp.float32)
    up_pre = jnp.einsum("erd,edf->erf", arrived, upward, preferred_element_type=jnp.float32)
    sigmoid_gate = jax.nn.sigmoid(gate_pre)
    activated = gate_pre * sigmoid_gate
    hidden = (activated * up_pre).astype(jnp.bfloat16)
    expert_out = jnp.einsum(
        "erf,edf->erd", hidden, lowering, preferred_element_type=jnp.float32
    ).astype(jnp.bfloat16)
    gating, upward, lowering = (
        lax.all_gather(gating_weight, "dp", axis=1, tiled=True),
        lax.all_gather(upward_weight, "dp", axis=1, tiled=True),
        lax.all_gather(down_weight, "dp", axis=1, tiled=True),
    )
    hidden_grad = jnp.einsum(
        "erd,edf->erf", arrived_grad, lowering, preferred_element_type=jnp.float32
    )
    gate_part = (
        hidden_grad * up_pre * sigmoid_gate * (1.0 + gate_pre * (1.0 - sigmoid_gate))
    ).astype(jnp.bfloat16)
    up_part = (hidden_grad * activated).astype(jnp.bfloat16)
    pair_grad = (
        jnp.einsum("erf,edf->erd", gate_part, gating, preferred_element_type=jnp.float32)
        + jnp.einsum("erf,edf->erd", up_part, upward, preferred_element_type=jnp.float32)
    ).astype(jnp.bfloat16)
    returned_out, returned_grad = (
        lax.all_to_all(expert_out, "expert", split_axis=1, concat_axis=0, tiled=True),
        lax.all_to_all(pair_grad, "expert", split_axis=1, concat_axis=0, tiled=True),
    )
    gating_term = jnp.einsum("erd,erf->edf", arrived, gate_part, preferred_element_type=jnp.float32)
    upward_term = jnp.einsum("erd,erf->edf", arrived, up_part, preferred_element_type=jnp.float32)
    down_term = jnp.einsum("erd,erf->edf", arrived_grad, hidden, preferred_element_type=jnp.float32)
    gating_grad, upward_grad, down_grad = (
        lax.psum_scatter(
            gating_term.astype(jnp.bfloat16), "dp", scatter_dimension=1, tiled=True
        ).astype(jnp.float32),
        lax.psum_scatter(
            upward_term.astype(jnp.bfloat16), "dp", scatter_dimension=1, tiled=True
        ).astype(jnp.float32),
        lax.psum_scatter(
            down_term.astype(jnp.bfloat16), "dp", scatter_dimension=1, tiled=True
        ).astype(jnp.float32),
    )
    returned_flat = returned_out.reshape(slot_total, -1)
    combined = jnp.zeros((row_count, returned_flat.shape[1]), jnp.float32)
    for choice_slot in range(TOPK):
        picker = placed[:, choice_slot, :].astype(jnp.bfloat16)
        picked = jnp.dot(picker, returned_flat, preferred_element_type=jnp.float32)
        combined = combined + gate_values[:, choice_slot][:, None] * picked
    layer_output = combined.astype(jnp.bfloat16)
    input_grad = jnp.dot(
        selector, returned_grad.reshape(slot_total, -1), preferred_element_type=jnp.float32
    ).astype(jnp.bfloat16)
    return (layer_output, input_grad, gating_grad, upward_grad, down_grad)


def solution(mesh):
    n_expert, n_dp = mesh.shape["expert"], mesh.shape["dp"]

    def program(*args):
        el = args[4].shape[0] // n_expert
        width = args[4].shape[1] // n_dp
        part = n_expert * n_dp // 4 * CAP
        fits = (
            n_dp == 4
            and n_expert == sum(map(len, GROUPS))
            and el % 2 == 0
            and el * CAP % 16 == 0
            and part % 16 == 0
            and width % 128 == 0
            and args[4].shape[2] % 128 == 0
            and args[0].shape[0] // (n_expert * n_dp) % 128 == 0
        )
        return jax.shard_map(
            shards if fits else general_shards,
            mesh=mesh,
            in_specs=(
                P(("expert", "dp"), None),
                P(("expert", "dp"), None),
                P(("expert", "dp"), None),
                P(("expert", "dp"), None),
                P("expert", "dp", None),
                P("expert", "dp", None),
                P("expert", "dp", None),
            ),
            out_specs=(
                P(("expert", "dp"), None),
                P(("expert", "dp"), None),
                P("expert", "dp", None),
                P("expert", "dp", None),
                P("expert", "dp", None),
            ),
            check_vma=False,
        )(*args)

    return program
```

```python
import functools
import jax
import jax.numpy as jnp
import numpy as np
from jax import lax
from jax.experimental import pallas as pl
from jax.experimental.pallas import tpu as pltpu
from jax.sharding import PartitionSpec as P

TOPK = 2
CAP = 6
MESH = pl.DeviceIdType.MESH
F32 = jnp.float32
BF16 = jnp.bfloat16
GROUPS = (((0, 0, 0), (1, 0, 0)), ((0, 1, 0), (1, 1, 0)), ((0, 0, 1), (1, 0, 1)), ((0, 1, 1), (1, 1, 1)))
RETURNS = (((0, 1, 1), (0, 0, 1), (0, 1, 0), (0, 0, 0)), ((1, 1, 1), (1, 0, 1), (1, 1, 0), (1, 0, 0)), ((2, 1, 1), (2, 0, 1), (2, 1, 0), (2, 0, 0)), ((3, 1, 1), (3, 0, 1), (3, 1, 0), (3, 0, 0)))
STEPS = (('cross', 0), ('send', ((0, 1, 0), (1, 1, 0), (0, 1, 1), (1, 1, 1), (0, 0, 0), (0, 0, 1), (1, 0, 0))), ('load', 0), ('swap', 0), ('send', ((1, 0, 1), (2, 1, 0), (2, 0, 0))), ('rows', 0), ('chip', 0), ('send', ((2, 1, 1), (2, 0, 1))), ('rows', 1), ('send', ((3, 1, 0), (3, 0, 0), (3, 1, 1), (3, 0, 1))), ('chip', 1), ('act', 0), ('rows', 2), ('chip', 2), ('act', 1), ('rows', 3), ('chip', 3), ('act', 2), ('act', 3))


def plane_kernel(
    n_expert, n_dp, el, width,
    tok_in, cot_in, routes_in, gates_in, perm_in, back_in, wg_ref, wu_ref, wd_ref,
    layer_ref, igrad_ref, dg, du, dd,
    tok_ref, cot_ref, routes_ref, gates_ref, perm_ref, back_ref,
    wg, wu, wd, halves, meta, direct, send, recv, rows, psend, pown, crecv, xsend, xrecv, hid,
    pre_ret, ret_send, ret, fin_send, fin_recv,
    in_send, in_recv, out_send, out_recv, pair_sem, swap_sem, local_sem,
):
    e_me = lax.axis_index("expert")
    d_me = lax.axis_index("dp")
    z_me, y_me = e_me // 2, lax.rem(e_me, 2)
    zh_me, zl_me = z_me // 2, lax.rem(z_me, 2)
    x_me, c_me = d_me // 2, lax.rem(d_me, 2)
    core_peer = (e_me, x_me * 2 + 1 - c_me)
    far_peer = (e_me, (1 - x_me) * 2 + c_me)
    per = n_dp * len(GROUPS[0])
    msg = el * CAP
    part = per * CAP
    half = el // 2
    some = half // 2
    ff = wg.shape[2]
    row_count = tok_ref.shape[0]
    slot_total = n_expert * msg
    wide = 2 * width
    plane = n_expert * 2

    def cols(index, size):
        return pl.ds(pl.multiple_of(index * size, size), size)

    def band(e):
        return pl.ds(pl.multiple_of(e * msg, msg), msg)

    input_copies = [
        pltpu.make_async_copy(src, dst, local_sem.at[5 + i])
        for i, (src, dst) in enumerate(
            (
                (routes_in, routes_ref), (gates_in, gates_ref), (tok_in, tok_ref), (cot_in, cot_ref),
                (perm_in, perm_ref), (back_in, back_ref),
            )
        )
    ]
    other_half = 1 - zh_me
    ends = [e_me] + [(other_half * 2 + lax.rem(zl_me + zl, 2)) * 2 + y_me for zl in range(2)]
    kind = lax.rem(zh_me + zl_me, 2)
    barrier = pltpu.get_barrier_semaphore()

    def greet(off, carry):
        other = lax.rem(e_me * 2 + c_me + off, plane)
        pl.semaphore_signal(
            barrier, inc=1, device_id=(other // 2, x_me * 2 + lax.rem(other, 2)), device_id_type=MESH
        )
        return carry

    lax.fori_loop(1, plane, greet, 0)
    across = [(e, (1 - x_me) * 2 + c) for e in ends for c in range(2)]
    for other in across:
        pl.semaphore_signal(barrier, inc=1, device_id=other, device_id_type=MESH)
    weight_copies = [
        pltpu.make_async_copy(src, dst, local_sem.at[i])
        for i, (src, dst) in enumerate(((wg_ref, wg), (wu_ref, wu), (wd_ref, wd)))
    ]
    for copy in input_copies:
        copy.start()
    for copy in weight_copies:
        copy.start()
    for copy in input_copies[:4]:
        copy.wait()

    expert_ids = lax.broadcasted_iota(jnp.int32, (n_expert * el, row_count), 0)
    named = [expert_ids == routes_ref[k : k + 1, :] for k in range(TOPK)]
    either = sum(jnp.where(n, 1.0, 0.0) for n in named).astype(BF16)
    square = (row_count, row_count)
    row_ids, col_ids = lax.broadcasted_iota(jnp.int32, square, 0), lax.broadcasted_iota(jnp.int32, square, 1)
    earlier = jnp.where(row_ids < col_ids, 1.0, 0.0).astype(BF16)
    before = jnp.dot(either, earlier, preferred_element_type=F32)
    for k in range(TOPK):
        position = jnp.sum(jnp.where(named[k], before, 0.0), axis=0, keepdims=True)
        meta[0, k : k + 1, :] = routes_ref[k : k + 1, :].astype(F32) * CAP + position
        meta[0, TOPK + k : TOPK + k + 1, :] = gates_ref[k : k + 1, :]
    meta[0, 2 * TOPK :, :] = jnp.zeros((meta.shape[1] - 2 * TOPK, row_count), F32)
    def swap_copy(i, src, dst):
        return pltpu.make_async_remote_copy(
            src_ref=src, dst_ref=dst, send_sem=swap_sem.at[0, i], recv_sem=swap_sem.at[1, i],
            device_id=far_peer, device_id_type=MESH,
        )

    swaps = [
        swap_copy(0, tok_ref.at[:, cols(1 - x_me, wide)], halves.at[0]),
        swap_copy(1, cot_ref.at[:, cols(1 - x_me, wide)], halves.at[1]),
        swap_copy(2, meta.at[0], meta.at[1]),
    ]
    slot_ids = lax.broadcasted_iota(jnp.int32, (slot_total, row_count), 0).astype(F32)

    def placed(s):
        return [slot_ids == meta[s, k : k + 1, :] for k in range(TOPK)]

    def fill(s, tok, cot):
        picks = placed(s)
        selector = sum(jnp.where(p, 1.0, 0.0) for p in picks).astype(BF16)
        weight = sum(
            jnp.where(p, meta[s, TOPK + k : TOPK + k + 1, :], 0.0) for k, p in enumerate(picks)
        )
        weight = jnp.sum(weight, axis=1, keepdims=True)
        send[s, 0] = jnp.dot(selector, tok, preferred_element_type=F32).astype(BF16)
        send[s, 1] = (jnp.dot(selector, cot, preferred_element_type=F32) * weight).astype(BF16)

    def place(g, i, j):
        far, zl, y = GROUPS[g][i]
        z = lax.rem(zh_me + far, 2) * 2 + lax.rem(zl_me + zl, 2)
        return z * 2 + lax.rem(y_me + y, 2), lax.rem(c_me + j, 2)

    def source(g, i, j):
        far, zl, y = GROUPS[g][i]
        if not far or g > 1:
            return place(g, i, j)
        z = other_half * 2 + lax.rem(other_half + zl, 2)
        return z * 2 + lax.rem(y_me + y, 2), lax.rem(c_me + j, 2)

    def label(g, i):
        far, zl, _ = GROUPS[g][i]
        return kind if far and g < 2 else g

    def sent_as(g, i):
        far, zl, _ = GROUPS[g][i]
        return lax.rem(other_half + zl + zl_me, 2) if far and g < 2 else g

    def home(g, i, j):
        return not any(GROUPS[g][i]) and j == 0

    def spot(i, s, c):
        return i * n_dp + (x_me if s == 0 else 1 - x_me) * 2 + c

    def fill_direct():
        other = cols(1 - x_me, wide)
        for i, e in enumerate(ends):
            ids = (lax.broadcasted_iota(jnp.int32, (msg, row_count), 0) + e * msg).astype(F32)
            picks = [ids == meta[0, k : k + 1, :] for k in range(TOPK)]
            selector = sum(jnp.where(p, 1.0, 0.0) for p in picks).astype(BF16)
            weight = sum(
                jnp.where(p, meta[0, TOPK + k : TOPK + k + 1, :], 0.0) for k, p in enumerate(picks)
            )
            weight = jnp.sum(weight, axis=1, keepdims=True)
            direct[i, 0] = jnp.dot(selector, tok_ref[:, other], preferred_element_type=F32).astype(BF16)
            direct[i, 1] = (
                jnp.dot(selector, cot_ref[:, other], preferred_element_type=F32) * weight
            ).astype(BF16)

    def message(where, at_me, there, src, dst, sems):
        return pltpu.make_async_remote_copy(
            src_ref=src,
            dst_ref=dst,
            send_sem=sems[0].at[at_me],
            recv_sem=sems[1].at[there],
            device_id=where,
            device_id_type=MESH,
        )

    def is_direct(g, i, s):
        return s == 1 and (g == 0 or (g == 1 and i == 1))

    def in_copy(g, i, s, j):
        e, c = place(g, i, j)
        group = label(g, i)
        at_me = g * per + spot(i, s, c)
        if is_direct(g, i, s):
            pos = spot(i, 0, c_me)
            return message(
                (e, (1 - x_me) * 2 + c), at_me, group * per + pos,
                direct.at[i + g, :, :, cols(c, width)], recv.at[group, pos], (in_send, in_recv),
            )
        pos = spot(i, s, c_me)
        src = send.at[s, :, band(e), cols(c, width)]
        if home(g, i, j):
            return pltpu.make_async_copy(src, recv.at[g, pos], local_sem.at[3 + s])
        return message(
            (e, x_me * 2 + c), at_me, group * per + pos, src, recv.at[group, pos], (in_send, in_recv)
        )

    def out_copy(g, i, s, j):
        e, c = source(g, i, j)
        src = ret_send.at[g, spot(i, s, c)]
        dst = ret.at[s, :, band(e_me), cols(c_me, width)]
        if home(g, i, j):
            return pltpu.make_async_copy(src, dst, local_sem.at[3 + s])
        return message(
            (e, x_me * 2 + c), g * per + spot(i, s, c), sent_as(g, i) * per + spot(i, s, c_me),
            src, dst, (out_send, out_recv),
        )

    def arrival(g, i, s, j, place_in, sems):
        e, c = place(g, i, j)
        return pltpu.make_async_remote_copy(
            src_ref=place_in,
            dst_ref=place_in,
            send_sem=sems[0].at[g * per + spot(i, s, c)],
            recv_sem=sems[1].at[g * per + spot(i, s, c)],
            device_id=(e, x_me * 2 + c),
            device_id_type=MESH,
        )

    def in_wait(g, i, s):
        for j in range(2):
            if home(g, i, j) and s == 0:
                in_copy(g, i, s, j).wait()
            else:
                c = place(g, i, j)[1]
                arrival(g, i, s, j, recv.at[g, spot(i, s, c)], (in_send, in_recv)).wait_recv()

    def out_wait(g, i, s):
        for j in range(2):
            if home(g, i, j):
                out_copy(g, i, s, j).wait()
            else:
                e, c = place(g, i, j)
                landed = ret.at[s, :, band(e), cols(c, width)]
                arrival(g, i, s, j, landed, (out_send, out_recv)).wait_recv()

    members = [(g, i) for g, group in enumerate(GROUPS) for i in range(len(group))]

    left = set()

    def await_left(messages):
        for g, i, s in messages:
            for j in range(2):
                if not home(g, i, j) or s:
                    in_copy(g, i, s, j).wait_send()
            left.add((g, i, s))

    def send_out(messages):
        for g, i, s in messages:
            for j in (1, 0):
                in_copy(g, i, s, j).start()

    fill(0, tok_ref[:, cols(x_me, wide)], cot_ref[:, cols(x_me, wide)])
    fill_direct()
    pl.semaphore_wait(barrier, plane - 1 + len(across))

    def pair_copy(k, src, dst, peer, stage):
        i = (stage * 4 + k[0]) * 2 + k[1]
        return pltpu.make_async_remote_copy(
            src_ref=src, dst_ref=dst, send_sem=pair_sem.at[0, i], recv_sem=pair_sem.at[1, i],
            device_id=peer, device_id_type=MESH,
        )

    def span(k):
        return pl.ds(k * part, part)

    def few(h, base=0):
        return pl.ds(base + h * some, some)

    parts = [(k, h) for k in range(4) for h in range(2)]
    core_copy = {
        (k, h): pair_copy((k, h), psend.at[k, few(h)], crecv.at[k, few(h)], core_peer, 0)
        for k, h in parts
    }
    far_copy = {
        (k, h): pair_copy((k, h), xsend.at[k, few(h)], xrecv.at[k, few(h)], far_peer, 1)
        for k, h in parts
    }
    hid_copy = {
        (k, h): pair_copy(
            (k, h), hid.at[few(h, c_me * half), span(k)], hid.at[few(h, c_me * half), span(k)], core_peer, 2
        )
        for k, h in parts
    }

    def partial(k, e, col):
        if col == 2:
            return jnp.dot(rows[e, span(k), width:], wd[e], preferred_element_type=F32)
        return jnp.dot(rows[e, span(k), :width], (wg, wu)[col][e], preferred_element_type=F32)

    def first_stage(k):
        for s in range(2):
            for i in range(len(GROUPS[k])):
                in_wait(k, i, s)
        for t in range(2):
            block = recv[k, :, t].reshape(per * msg, width)
            moved = jnp.dot(perm_ref[...], block, preferred_element_type=F32).astype(BF16)
            rows[:, k * part : (k + 1) * part, t * width : (t + 1) * width] = moved.reshape(
                el, part, width
            )

        def other(j, carry):
            for col in range(3):
                psend[k, j, :, col * ff : (col + 1) * ff] = partial(
                    k, (1 - c_me) * half + j, col
                ).astype(BF16)
            return carry

        for h in range(2):
            lax.fori_loop(h * some, (h + 1) * some, other, 0, unroll=True)
            core_copy[k, h].start()

        def own(j, carry):
            for col in range(3):
                pown[k, j, :, col * ff : (col + 1) * ff] = partial(k, c_me * half + j, col)
            return carry

        lax.fori_loop(0, half, own, 0, unroll=True)

    def chip_sum(k):
        def body(j, carry):
            s = pown[k, j] + crecv[k, j].astype(F32)
            pown[k, j] = s
            xsend[k, j] = s.astype(BF16)
            return carry

        for h in range(2):
            core_copy[k, h].wait_recv()
            lax.fori_loop(h * some, (h + 1) * some, body, 0)
            far_copy[k, h].start()

    def middle(k, h):
        far_copy[k, h].wait_recv()

        def body(j, carry):
            s = pown[k, j] + xrecv[k, j].astype(F32)
            gate_pre, up_pre, hidden_grad = s[:, :ff], s[:, ff : 2 * ff], s[:, 2 * ff :]
            sig = jax.nn.sigmoid(gate_pre)
            act = gate_pre * sig
            e = c_me * half + j
            hid[e, span(k), :ff] = (act * up_pre).astype(BF16)
            hid[e, span(k), ff : 2 * ff] = (
                hidden_grad * up_pre * sig * (1.0 + gate_pre * (1.0 - sig))
            ).astype(BF16)
            hid[e, span(k), 2 * ff :] = (hidden_grad * act).astype(BF16)
            return carry

        lax.fori_loop(h * some, (h + 1) * some, body, 0)
        hid_copy[k, h].start()

    last = (((1,), (1,)), ((), ()))
    first = (((0,), (0,)), ((), ()))

    def last_stage(k):
        def body(j, carry, base):
            e = base + j
            h = hid[e, span(k)]
            pre_ret[0, e] = lax.dot_general(
                h[:, :ff], wd[e], last, preferred_element_type=F32
            ).astype(BF16)
            pre_ret[1, e] = (
                lax.dot_general(h[:, ff : 2 * ff], wg[e], last, preferred_element_type=F32)
                + lax.dot_general(h[:, 2 * ff :], wu[e], last, preferred_element_type=F32)
            ).astype(BF16)
            return carry

        for h in range(2):
            middle(k, h)
            lax.fori_loop(
                h * some, (h + 1) * some, functools.partial(body, base=c_me * half), 0, unroll=True
            )
        for h in range(2):
            hid_copy[k, h].wait_recv()
            lax.fori_loop(
                h * some, (h + 1) * some, functools.partial(body, base=(1 - c_me) * half), 0, unroll=True
            )
        for t in range(2):
            block = pre_ret[t].reshape(el * part, width)
            moved = jnp.dot(back_ref[...], block, preferred_element_type=F32).astype(BF16)
            ret_send[k, :, t] = moved.reshape(per, msg, width)
        for g, i, s in RETURNS[k]:
            for j in (1, 0):
                out_copy(g, i, s, j).start()

    def load(_):
        for copy in input_copies[4:]:
            copy.wait()
        for copy in weight_copies:
            copy.wait()

    def swap_out(_):
        for copy in swaps:
            copy.start()

    def swap_in(_):
        for copy in swaps:
            copy.wait_recv()
        fill(1, halves[0], halves[1])

    work = dict(send=send_out, left=await_left, load=load, rows=first_stage, cross=swap_out, swap=swap_in, chip=chip_sum, act=last_stage)
    for step, k in STEPS:
        work[step](k)

    def grads(e, carry):
        tok, grad = rows[e, :, :width], rows[e, :, width:]
        h = hid[e]
        dg[e] = lax.dot_general(tok, h[:, ff : 2 * ff], first, preferred_element_type=F32)
        du[e] = lax.dot_general(tok, h[:, 2 * ff :], first, preferred_element_type=F32)
        dd[e] = lax.dot_general(grad, h[:, :ff], first, preferred_element_type=F32)
        return carry

    lax.fori_loop(0, half, grads, 0)

    def combine(s):
        picks = [jnp.where(p, 1.0, 0.0) for p in placed(s)]
        out = 0.0
        for k in range(TOPK):
            gate = jnp.sum(
                jnp.where(row_ids == col_ids, meta[s, TOPK + k : TOPK + k + 1, :], 0.0),
                axis=1,
                keepdims=True,
            )
            picked = lax.dot_general(
                picks[k].astype(BF16), ret[s, 0], first, preferred_element_type=F32
            )
            out = out + gate * picked
        grad = lax.dot_general(
            sum(picks).astype(BF16), ret[s, 1], first, preferred_element_type=F32
        )
        return out.astype(BF16), grad.astype(BF16)

    fin_copy = [swap_copy(3 + i, fin_send.at[i], fin_recv.at[i]) for i in range(2)]
    for s in (1, 0):
        for g, i in members:
            out_wait(g, i, s)
        out, grad = combine(s)
        if s == 1:
            fin_send[0] = out
            fin_send[1] = grad
            for copy in fin_copy:
                copy.start()
            lax.fori_loop(half, el, grads, 0)
        else:
            layer_ref[:, cols(x_me, wide)] = out
            igrad_ref[:, cols(x_me, wide)] = grad
    for copy in swaps:
        copy.wait_send()
    for k in range(4):
        for i in range(len(GROUPS[k])):
            for s in range(2):
                for j in range(2):
                    if (k, i, s) not in left and (s or not home(k, i, j)):
                        in_copy(k, i, s, j).wait_send()
                    if not home(k, i, j):
                        out_copy(k, i, s, j).wait_send()
        for h in range(2):
            core_copy[k, h].wait_send()
            far_copy[k, h].wait_send()
            hid_copy[k, h].wait_send()

    for copy in fin_copy:
        copy.wait()
    layer_ref[:, cols(1 - x_me, wide)] = fin_recv[0]
    igrad_ref[:, cols(1 - x_me, wide)] = fin_recv[1]


def store_kernel(layer, igrad, dg, du, dd, layer_out, igrad_out, dg_out, du_out, dd_out, sem):
    pairs = [
        (src.at[e], dst.at[e])
        for e in range(dg.shape[0])
        for src, dst in ((dg, dg_out), (du, du_out), (dd, dd_out))
    ]
    pairs += [(layer, layer_out), (igrad, igrad_out)]
    copies = [pltpu.make_async_copy(src, dst, sem.at[i]) for i, (src, dst) in enumerate(pairs)]
    for copy in copies:
        copy.start()
    for copy in copies:
        copy.wait()


def shards(tokens, routes, gate_values, cotangent, gating_weight, upward_weight, down_weight):
    n_expert, n_dp = lax.axis_size("expert"), lax.axis_size("dp")
    el, width, ff = gating_weight.shape
    row_count = tokens.shape[0]
    per = n_expert * n_dp // 4
    msg = el * CAP
    part = per * CAP
    slots = 4 * part
    half = el // 2
    wide = 3 * ff
    spot = np.arange(per * msg)
    e, s, c = spot // part, spot % part // CAP, spot % CAP
    perm = np.zeros((per * msg, per * msg), np.float32)
    perm[spot, s * msg + e * CAP + c] = 1.0
    hbm = pl.BlockSpec(memory_space=pltpu.HBM)
    vmem = pl.BlockSpec(memory_space=pltpu.VMEM)
    weight_shape = gating_weight.shape
    layer_output, input_grad, dg, du, dd = pl.pallas_call(
        functools.partial(plane_kernel, n_expert, n_dp, el, width),
        out_shape=(
            pltpu.VMEM(tokens.shape, BF16),
            pltpu.VMEM(tokens.shape, BF16),
            pltpu.VMEM(weight_shape, F32),
            pltpu.VMEM(weight_shape, F32),
            pltpu.VMEM(weight_shape, F32),
        ),
        in_specs=[hbm] * 9,
        out_specs=[vmem] * 5,
        scratch_shapes=[
            pltpu.VMEM(tokens.shape, BF16),
            pltpu.VMEM(tokens.shape, BF16),
            pltpu.VMEM((TOPK, row_count), jnp.int32),
            pltpu.VMEM((TOPK, row_count), F32),
            pltpu.VMEM(perm.shape, BF16),
            pltpu.VMEM(perm.shape, BF16),
            pltpu.VMEM(weight_shape, BF16),
            pltpu.VMEM(weight_shape, BF16),
            pltpu.VMEM(weight_shape, BF16),
            pltpu.VMEM((2, row_count, 2 * width), BF16),
            pltpu.VMEM((2, 8, row_count), F32),
            pltpu.VMEM((3, 2, msg, 2 * width), BF16),
            pltpu.VMEM((2, 2, n_expert * msg, 2 * width), BF16),
            pltpu.VMEM((4, per, 2, msg, width), BF16),
            pltpu.VMEM((el, slots, 2 * width), BF16),
            pltpu.VMEM((4, half, part, wide), BF16),
            pltpu.VMEM((4, half, part, wide), F32),
            pltpu.VMEM((4, half, part, wide), BF16),
            pltpu.VMEM((4, half, part, wide), BF16),
            pltpu.VMEM((4, half, part, wide), BF16),
            pltpu.VMEM((el, slots, wide), BF16),
            pltpu.VMEM((2, el, part, width), BF16),
            pltpu.VMEM((4, per, 2, msg, width), BF16),
            pltpu.VMEM((2, 2, n_expert * msg, 2 * width), BF16),
            pltpu.VMEM((2, row_count, 2 * width), BF16),
            pltpu.VMEM((2, row_count, 2 * width), BF16),
            pltpu.SemaphoreType.DMA((4 * per,)),
            pltpu.SemaphoreType.DMA((4 * per,)),
            pltpu.SemaphoreType.DMA((4 * per,)),
            pltpu.SemaphoreType.DMA((4 * per,)),
            pltpu.SemaphoreType.DMA((2, 24)),
            pltpu.SemaphoreType.DMA((2, 5)),
            pltpu.SemaphoreType.DMA((11,)),
        ],
        compiler_params=pltpu.CompilerParams(
            collective_id=0, has_side_effects=True, vmem_limit_bytes=44 * 1024 * 1024
        ),
    )(
        *(
            pltpu.with_memory_space_constraint(a, pltpu.HBM)
            for a in (
                tokens,
                cotangent,
                routes.T,
                gate_values.T,
                jnp.asarray(perm, BF16),
                jnp.asarray(perm.T, BF16),
                gating_weight,
                upward_weight,
                down_weight,
            )
        )
    )
    results = (layer_output, input_grad, dg, du, dd)
    return pl.pallas_call(
        store_kernel,
        out_shape=tuple(jax.ShapeDtypeStruct(r.shape, r.dtype) for r in results),
        in_specs=[vmem] * 5,
        out_specs=[hbm] * 5,
        scratch_shapes=[pltpu.SemaphoreType.DMA((2 + 3 * el,))],
        compiler_params=pltpu.CompilerParams(vmem_limit_bytes=16 * 1024 * 1024),
    )(*results)


def general_shards(tokens, routes, gate_values, cotangent, gating_weight, upward_weight, down_weight):
    expert_total = gating_weight.shape[0] * lax.axis_size("expert")
    row_count = tokens.shape[0]
    slot_total = expert_total * CAP
    flat_routes = routes.reshape(-1)
    onehot = (flat_routes[:, None] == jnp.arange(expert_total, dtype=jnp.int32)[None, :]).astype(
        jnp.int32
    )
    position = jnp.sum((jnp.cumsum(onehot, axis=0) - onehot) * onehot, axis=1)
    slot_index = flat_routes * CAP + position
    placed = (slot_index[:, None] == jnp.arange(slot_total, dtype=jnp.int32)[None, :]).astype(
        jnp.float32
    )
    placed = placed.reshape(row_count, TOPK, slot_total)
    selector = jnp.sum(placed, axis=1).astype(jnp.bfloat16)
    slot_gate = jnp.sum(placed * gate_values[:, :, None], axis=(0, 1))
    contract = (((0,), (0,)), ((), ()))
    send_rows = lax.dot_general(selector, tokens, contract, preferred_element_type=jnp.float32)
    send_rows = send_rows.astype(jnp.bfloat16).reshape(expert_total, CAP, -1)
    slot_cotangent = lax.dot_general(
        selector, cotangent, contract, preferred_element_type=jnp.float32
    )
    send_grads = (
        (slot_cotangent * slot_gate[:, None]).astype(jnp.bfloat16).reshape(expert_total, CAP, -1)
    )
    arrived, arrived_grad = (
        lax.all_to_all(send_rows, "expert", split_axis=0, concat_axis=1, tiled=True),
        lax.all_to_all(send_grads, "expert", split_axis=0, concat_axis=1, tiled=True),
    )
    gating, upward, lowering = (
        lax.all_gather(gating_weight, "dp", axis=1, tiled=True),
        lax.all_gather(upward_weight, "dp", axis=1, tiled=True),
        lax.all_gather(down_weight, "dp", axis=1, tiled=True),
    )
    gate_pre = jnp.einsum("erd,edf->erf", arrived, gating, preferred_element_type=jnp.float32)
    up_pre = jnp.einsum("erd,edf->erf", arrived, upward, preferred_element_type=jnp.float32)
    sigmoid_gate = jax.nn.sigmoid(gate_pre)
    activated = gate_pre * sigmoid_gate
    hidden = (activated * up_pre).astype(jnp.bfloat16)
    expert_out = jnp.einsum(
        "erf,edf->erd", hidden, lowering, preferred_element_type=jnp.float32
    ).astype(jnp.bfloat16)
    gating, upward, lowering = (
        lax.all_gather(gating_weight, "dp", axis=1, tiled=True),
        lax.all_gather(upward_weight, "dp", axis=1, tiled=True),
        lax.all_gather(down_weight, "dp", axis=1, tiled=True),
    )
    hidden_grad = jnp.einsum(
        "erd,edf->erf", arrived_grad, lowering, preferred_element_type=jnp.float32
    )
    gate_part = (
        hidden_grad * up_pre * sigmoid_gate * (1.0 + gate_pre * (1.0 - sigmoid_gate))
    ).astype(jnp.bfloat16)
    up_part = (hidden_grad * activated).astype(jnp.bfloat16)
    pair_grad = (
        jnp.einsum("erf,edf->erd", gate_part, gating, preferred_element_type=jnp.float32)
        + jnp.einsum("erf,edf->erd", up_part, upward, preferred_element_type=jnp.float32)
    ).astype(jnp.bfloat16)
    returned_out, returned_grad = (
        lax.all_to_all(expert_out, "expert", split_axis=1, concat_axis=0, tiled=True),
        lax.all_to_all(pair_grad, "expert", split_axis=1, concat_axis=0, tiled=True),
    )
    gating_term = jnp.einsum("erd,erf->edf", arrived, gate_part, preferred_element_type=jnp.float32)
    upward_term = jnp.einsum("erd,erf->edf", arrived, up_part, preferred_element_type=jnp.float32)
    down_term = jnp.einsum("erd,erf->edf", arrived_grad, hidden, preferred_element_type=jnp.float32)
    gating_grad, upward_grad, down_grad = (
        lax.psum_scatter(
            gating_term.astype(jnp.bfloat16), "dp", scatter_dimension=1, tiled=True
        ).astype(jnp.float32),
        lax.psum_scatter(
            upward_term.astype(jnp.bfloat16), "dp", scatter_dimension=1, tiled=True
        ).astype(jnp.float32),
        lax.psum_scatter(
            down_term.astype(jnp.bfloat16), "dp", scatter_dimension=1, tiled=True
        ).astype(jnp.float32),
    )
    returned_flat = returned_out.reshape(slot_total, -1)
    combined = jnp.zeros((row_count, returned_flat.shape[1]), jnp.float32)
    for choice_slot in range(TOPK):
        picker = placed[:, choice_slot, :].astype(jnp.bfloat16)
        picked = jnp.dot(picker, returned_flat, preferred_element_type=jnp.float32)
        combined = combined + gate_values[:, choice_slot][:, None] * picked
    layer_output = combined.astype(jnp.bfloat16)
    input_grad = jnp.dot(
        selector, returned_grad.reshape(slot_total, -1), preferred_element_type=jnp.float32
    ).astype(jnp.bfloat16)
    return (layer_output, input_grad, gating_grad, upward_grad, down_grad)


def solution(mesh):
    n_expert, n_dp = mesh.shape["expert"], mesh.shape["dp"]

    def program(*args):
        el = args[4].shape[0] // n_expert
        width = args[4].shape[1] // n_dp
        part = n_expert * n_dp // 4 * CAP
        fits = (
            n_dp == 4
            and n_expert == sum(map(len, GROUPS))
            and el % 4 == 0
            and el * CAP % 16 == 0
            and part % 16 == 0
            and width % 128 == 0
            and args[4].shape[2] % 128 == 0
            and args[0].shape[0] // (n_expert * n_dp) % 128 == 0
        )
        return jax.shard_map(
            shards if fits else general_shards,
            mesh=mesh,
            in_specs=(
                P(("expert", "dp"), None),
                P(("expert", "dp"), None),
                P(("expert", "dp"), None),
                P(("expert", "dp"), None),
                P("expert", "dp", None),
                P("expert", "dp", None),
                P("expert", "dp", None),
            ),
            out_specs=(
                P(("expert", "dp"), None),
                P(("expert", "dp"), None),
                P("expert", "dp", None),
                P("expert", "dp", None),
                P("expert", "dp", None),
            ),
            check_vma=False,
        )(*args)

    return program
```

```python
import functools
import jax
import jax.numpy as jnp
import numpy as np
from jax import lax
from jax.experimental import pallas as pl
from jax.experimental.pallas import tpu as pltpu
from jax.sharding import PartitionSpec as P

TOPK = 2
CAP = 6
MESH = pl.DeviceIdType.MESH
F32 = jnp.float32
BF16 = jnp.bfloat16
GROUPS = (((0, 0, 0), (1, 0, 0)), ((0, 1, 0), (1, 1, 0)), ((0, 0, 1), (1, 0, 1)), ((0, 1, 1), (1, 1, 1)))
RETURNS = (((0, 1, 1), (0, 0, 1), (0, 1, 0), (0, 0, 0)), ((1, 1, 1), (1, 0, 1), (1, 1, 0), (1, 0, 0)), ((2, 1, 1), (2, 0, 1), (2, 1, 0), (2, 0, 0)), ((3, 1, 1), (3, 0, 1), (3, 1, 0), (3, 0, 0)))
STEPS = (('cross', 0), ('send', ((0, 1, 0), (1, 1, 0), (0, 1, 1), (1, 1, 1), (0, 0, 0), (0, 0, 1), (1, 0, 0))), ('load', 0), ('swap', 0), ('send', ((1, 0, 1), (2, 1, 0), (2, 0, 0))), ('rows', 0), ('chip', 0), ('send', ((2, 1, 1), (2, 0, 1))), ('rows', 1), ('send', ((3, 1, 0), (3, 0, 0), (3, 1, 1), (3, 0, 1))), ('chip', 1), ('act', 0), ('rows', 2), ('chip', 2), ('act', 1), ('rows', 3), ('chip', 3), ('act', 2), ('act', 3))


def plane_kernel(
    n_expert, n_dp, el, width,
    tok_in, cot_in, routes_in, gates_in, perm_in, back_in, wg_ref, wu_ref, wd_ref,
    layer_ref, igrad_ref, dg, du, dd,
    tok_ref, cot_ref, routes_ref, gates_ref, perm_ref, back_ref,
    wg, wu, wd, halves, meta, direct, send, recv, rows, psend, pown, crecv, xsend, xrecv, hid,
    pre_ret, ret_send, ret, fin_send, fin_recv,
    in_send, in_recv, out_send, out_recv, pair_sem, swap_sem, local_sem,
):
    e_me = lax.axis_index("expert")
    d_me = lax.axis_index("dp")
    z_me, y_me = e_me // 2, lax.rem(e_me, 2)
    zh_me, zl_me = z_me // 2, lax.rem(z_me, 2)
    x_me, c_me = d_me // 2, lax.rem(d_me, 2)
    core_peer = (e_me, x_me * 2 + 1 - c_me)
    far_peer = (e_me, (1 - x_me) * 2 + c_me)
    per = n_dp * len(GROUPS[0])
    msg = el * CAP
    part = per * CAP
    half = el // 2
    some = half // 2
    ff = wg.shape[2]
    row_count = tok_ref.shape[0]
    slot_total = n_expert * msg
    wide = 2 * width
    plane = n_expert * 2

    def cols(index, size):
        return pl.ds(pl.multiple_of(index * size, size), size)

    def band(e):
        return pl.ds(pl.multiple_of(e * msg, msg), msg)

    input_copies = [
        pltpu.make_async_copy(src, dst, local_sem.at[5 + i])
        for i, (src, dst) in enumerate(
            (
                (routes_in, routes_ref), (gates_in, gates_ref), (tok_in, tok_ref), (cot_in, cot_ref),
                (perm_in, perm_ref), (back_in, back_ref),
            )
        )
    ]
    other_half = 1 - zh_me
    ends = [e_me] + [(other_half * 2 + lax.rem(zl_me + zl, 2)) * 2 + y_me for zl in range(2)]
    kind = lax.rem(zh_me + zl_me, 2)
    barrier = pltpu.get_barrier_semaphore()

    def greet(off, carry):
        other = lax.rem(e_me * 2 + c_me + off, plane)
        pl.semaphore_signal(
            barrier, inc=1, device_id=(other // 2, x_me * 2 + lax.rem(other, 2)), device_id_type=MESH
        )
        return carry

    lax.fori_loop(1, plane, greet, 0)
    across = [(e, (1 - x_me) * 2 + c) for e in ends for c in range(2)]
    for other in across:
        pl.semaphore_signal(barrier, inc=1, device_id=other, device_id_type=MESH)
    weight_copies = [
        pltpu.make_async_copy(src, dst, local_sem.at[i])
        for i, (src, dst) in enumerate(((wg_ref, wg), (wu_ref, wu), (wd_ref, wd)))
    ]
    for copy in input_copies:
        copy.start()
    for copy in weight_copies:
        copy.start()
    for copy in input_copies[:4]:
        copy.wait()

    expert_ids = lax.broadcasted_iota(jnp.int32, (n_expert * el, row_count), 0)
    named = [expert_ids == routes_ref[k : k + 1, :] for k in range(TOPK)]
    either = sum(jnp.where(n, 1.0, 0.0) for n in named).astype(BF16)
    square = (row_count, row_count)
    row_ids, col_ids = lax.broadcasted_iota(jnp.int32, square, 0), lax.broadcasted_iota(jnp.int32, square, 1)
    earlier = jnp.where(row_ids < col_ids, 1.0, 0.0).astype(BF16)
    before = jnp.dot(either, earlier, preferred_element_type=F32)
    for k in range(TOPK):
        position = jnp.sum(jnp.where(named[k], before, 0.0), axis=0, keepdims=True)
        meta[0, k : k + 1, :] = routes_ref[k : k + 1, :].astype(F32) * CAP + position
        meta[0, TOPK + k : TOPK + k + 1, :] = gates_ref[k : k + 1, :]
    meta[0, 2 * TOPK :, :] = jnp.zeros((meta.shape[1] - 2 * TOPK, row_count), F32)
    def swap_copy(i, src, dst):
        return pltpu.make_async_remote_copy(
            src_ref=src, dst_ref=dst, send_sem=swap_sem.at[0, i], recv_sem=swap_sem.at[1, i],
            device_id=far_peer, device_id_type=MESH,
        )

    swaps = [
        swap_copy(0, tok_ref.at[:, cols(1 - x_me, wide)], halves.at[0]),
        swap_copy(1, cot_ref.at[:, cols(1 - x_me, wide)], halves.at[1]),
        swap_copy(2, meta.at[0], meta.at[1]),
    ]
    slot_ids = lax.broadcasted_iota(jnp.int32, (slot_total, row_count), 0).astype(F32)

    def placed(s):
        return [slot_ids == meta[s, k : k + 1, :] for k in range(TOPK)]

    def fill(s, tok, cot):
        picks = placed(s)
        selector = sum(jnp.where(p, 1.0, 0.0) for p in picks).astype(BF16)
        weight = sum(
            jnp.where(p, meta[s, TOPK + k : TOPK + k + 1, :], 0.0) for k, p in enumerate(picks)
        )
        weight = jnp.sum(weight, axis=1, keepdims=True)
        send[s, 0] = jnp.dot(selector, tok, preferred_element_type=F32).astype(BF16)
        send[s, 1] = (jnp.dot(selector, cot, preferred_element_type=F32) * weight).astype(BF16)

    def place(g, i, j):
        far, zl, y = GROUPS[g][i]
        z = lax.rem(zh_me + far, 2) * 2 + lax.rem(zl_me + zl, 2)
        return z * 2 + lax.rem(y_me + y, 2), lax.rem(c_me + j, 2)

    def source(g, i, j):
        far, zl, y = GROUPS[g][i]
        if not far or g > 1:
            return place(g, i, j)
        z = other_half * 2 + lax.rem(other_half + zl, 2)
        return z * 2 + lax.rem(y_me + y, 2), lax.rem(c_me + j, 2)

    def label(g, i):
        far, zl, _ = GROUPS[g][i]
        return kind if far and g < 2 else g

    def sent_as(g, i):
        far, zl, _ = GROUPS[g][i]
        return lax.rem(other_half + zl + zl_me, 2) if far and g < 2 else g

    def home(g, i, j):
        return not any(GROUPS[g][i]) and j == 0

    def spot(i, s, c):
        return i * n_dp + (x_me if s == 0 else 1 - x_me) * 2 + c

    def fill_direct():
        other = cols(1 - x_me, wide)
        for i, e in enumerate(ends):
            ids = (lax.broadcasted_iota(jnp.int32, (msg, row_count), 0) + e * msg).astype(F32)
            picks = [ids == meta[0, k : k + 1, :] for k in range(TOPK)]
            selector = sum(jnp.where(p, 1.0, 0.0) for p in picks).astype(BF16)
            weight = sum(
                jnp.where(p, meta[0, TOPK + k : TOPK + k + 1, :], 0.0) for k, p in enumerate(picks)
            )
            weight = jnp.sum(weight, axis=1, keepdims=True)
            direct[i, 0] = jnp.dot(selector, tok_ref[:, other], preferred_element_type=F32).astype(BF16)
            direct[i, 1] = (
                jnp.dot(selector, cot_ref[:, other], preferred_element_type=F32) * weight
            ).astype(BF16)

    def message(where, at_me, there, src, dst, sems):
        return pltpu.make_async_remote_copy(
            src_ref=src,
            dst_ref=dst,
            send_sem=sems[0].at[at_me],
            recv_sem=sems[1].at[there],
            device_id=where,
            device_id_type=MESH,
        )

    def is_direct(g, i, s):
        return s == 1 and (g == 0 or (g == 1 and i == 1))

    def in_copy(g, i, s, j):
        e, c = place(g, i, j)
        group = label(g, i)
        at_me = g * per + spot(i, s, c)
        if is_direct(g, i, s):
            pos = spot(i, 0, c_me)
            return message(
                (e, (1 - x_me) * 2 + c), at_me, group * per + pos,
                direct.at[i + g, :, :, cols(c, width)], recv.at[group, pos], (in_send, in_recv),
            )
        pos = spot(i, s, c_me)
        src = send.at[s, :, band(e), cols(c, width)]
        if home(g, i, j):
            return pltpu.make_async_copy(src, recv.at[g, pos], local_sem.at[3 + s])
        return message(
            (e, x_me * 2 + c), at_me, group * per + pos, src, recv.at[group, pos], (in_send, in_recv)
        )

    def out_copy(g, i, s, j):
        e, c = source(g, i, j)
        src = ret_send.at[g, spot(i, s, c)]
        dst = ret.at[s, :, band(e_me), cols(c_me, width)]
        if home(g, i, j):
            return pltpu.make_async_copy(src, dst, local_sem.at[3 + s])
        return message(
            (e, x_me * 2 + c), g * per + spot(i, s, c), sent_as(g, i) * per + spot(i, s, c_me),
            src, dst, (out_send, out_recv),
        )

    def arrival(g, i, s, j, place_in, sems):
        e, c = place(g, i, j)
        return pltpu.make_async_remote_copy(
            src_ref=place_in,
            dst_ref=place_in,
            send_sem=sems[0].at[g * per + spot(i, s, c)],
            recv_sem=sems[1].at[g * per + spot(i, s, c)],
            device_id=(e, x_me * 2 + c),
            device_id_type=MESH,
        )

    def in_wait(g, i, s):
        for j in range(2):
            if home(g, i, j) and s == 0:
                in_copy(g, i, s, j).wait()
            else:
                c = place(g, i, j)[1]
                arrival(g, i, s, j, recv.at[g, spot(i, s, c)], (in_send, in_recv)).wait_recv()

    def out_wait(g, i, s):
        for j in range(2):
            if home(g, i, j):
                out_copy(g, i, s, j).wait()
            else:
                e, c = place(g, i, j)
                landed = ret.at[s, :, band(e), cols(c, width)]
                arrival(g, i, s, j, landed, (out_send, out_recv)).wait_recv()

    members = [(g, i) for g, group in enumerate(GROUPS) for i in range(len(group))]

    left = set()

    def await_left(messages):
        for g, i, s in messages:
            for j in range(2):
                if not home(g, i, j) or s:
                    in_copy(g, i, s, j).wait_send()
            left.add((g, i, s))

    def send_out(messages):
        for g, i, s in messages:
            for j in (1, 0):
                in_copy(g, i, s, j).start()

    fill(0, tok_ref[:, cols(x_me, wide)], cot_ref[:, cols(x_me, wide)])
    fill_direct()
    pl.semaphore_wait(barrier, plane - 1 + len(across))

    def pair_copy(k, src, dst, peer, stage):
        i = (stage * 4 + k[0]) * 2 + k[1]
        return pltpu.make_async_remote_copy(
            src_ref=src, dst_ref=dst, send_sem=pair_sem.at[0, i], recv_sem=pair_sem.at[1, i],
            device_id=peer, device_id_type=MESH,
        )

    def span(k):
        return pl.ds(k * part, part)

    def few(h, base=0):
        return pl.ds(base + h * some, some)

    parts = [(k, h) for k in range(4) for h in range(2)]
    core_copy = {
        (k, h): pair_copy((k, h), psend.at[k, few(h)], crecv.at[k, few(h)], core_peer, 0)
        for k, h in parts
    }
    far_copy = {
        (k, h): pair_copy((k, h), xsend.at[k, few(h)], xrecv.at[k, few(h)], far_peer, 1)
        for k, h in parts
    }
    hid_copy = {
        (k, h): pair_copy(
            (k, h), hid.at[few(h, c_me * half), span(k)], hid.at[few(h, c_me * half), span(k)], core_peer, 2
        )
        for k, h in parts
    }

    def partial(k, e, col):
        if col == 2:
            return jnp.dot(rows[e, span(k), width:], wd[e], preferred_element_type=F32)
        return jnp.dot(rows[e, span(k), :width], (wg, wu)[col][e], preferred_element_type=F32)

    def first_stage(k):
        for s in range(2):
            for i in range(len(GROUPS[k])):
                in_wait(k, i, s)
        for t in range(2):
            block = recv[k, :, t].reshape(per * msg, width)
            moved = jnp.dot(perm_ref[...], block, preferred_element_type=F32).astype(BF16)
            rows[:, k * part : (k + 1) * part, t * width : (t + 1) * width] = moved.reshape(
                el, part, width
            )

        def other(j, carry):
            for col in range(3):
                psend[k, j, :, col * ff : (col + 1) * ff] = partial(
                    k, (1 - c_me) * half + j, col
                ).astype(BF16)
            return carry

        for h in range(2):
            lax.fori_loop(h * some, (h + 1) * some, other, 0, unroll=True)
            core_copy[k, h].start()

        def own(j, carry):
            for col in range(3):
                pown[k, j, :, col * ff : (col + 1) * ff] = partial(k, c_me * half + j, col)
            return carry

        lax.fori_loop(0, half, own, 0, unroll=True)

    def chip_sum(k):
        def body(j, carry):
            s = pown[k, j] + crecv[k, j].astype(F32)
            pown[k, j] = s
            xsend[k, j] = s.astype(BF16)
            return carry

        for h in range(2):
            core_copy[k, h].wait_recv()
            lax.fori_loop(h * some, (h + 1) * some, body, 0)
            far_copy[k, h].start()

    def middle(k, h):
        far_copy[k, h].wait_recv()

        def body(j, carry):
            s = pown[k, j] + xrecv[k, j].astype(F32)
            gate_pre, up_pre, hidden_grad = s[:, :ff], s[:, ff : 2 * ff], s[:, 2 * ff :]
            sig = jax.nn.sigmoid(gate_pre)
            act = gate_pre * sig
            e = c_me * half + j
            hid[e, span(k), :ff] = (act * up_pre).astype(BF16)
            hid[e, span(k), ff : 2 * ff] = (
                hidden_grad * up_pre * sig * (1.0 + gate_pre * (1.0 - sig))
            ).astype(BF16)
            hid[e, span(k), 2 * ff :] = (hidden_grad * act).astype(BF16)
            return carry

        lax.fori_loop(h * some, (h + 1) * some, body, 0)
        hid_copy[k, h].start()

    last = (((1,), (1,)), ((), ()))
    first = (((0,), (0,)), ((), ()))

    def last_stage(k):
        def body(j, carry, base):
            e = base + j
            h = hid[e, span(k)]
            pre_ret[0, e] = lax.dot_general(
                h[:, :ff], wd[e], last, preferred_element_type=F32
            ).astype(BF16)
            pre_ret[1, e] = (
                lax.dot_general(h[:, ff : 2 * ff], wg[e], last, preferred_element_type=F32)
                + lax.dot_general(h[:, 2 * ff :], wu[e], last, preferred_element_type=F32)
            ).astype(BF16)
            return carry

        for h in range(2):
            middle(k, h)
            lax.fori_loop(
                h * some, (h + 1) * some, functools.partial(body, base=c_me * half), 0, unroll=True
            )
        for h in range(2):
            hid_copy[k, h].wait_recv()
            lax.fori_loop(
                h * some, (h + 1) * some, functools.partial(body, base=(1 - c_me) * half), 0, unroll=True
            )
        for t in range(2):
            block = pre_ret[t].reshape(el * part, width)
            moved = jnp.dot(back_ref[...], block, preferred_element_type=F32).astype(BF16)
            ret_send[k, :, t] = moved.reshape(per, msg, width)
        for g, i, s in RETURNS[k]:
            for j in (1, 0):
                out_copy(g, i, s, j).start()

    def load(_):
        for copy in input_copies[4:]:
            copy.wait()
        for copy in weight_copies:
            copy.wait()

    def swap_out(_):
        for copy in swaps:
            copy.start()

    def swap_in(_):
        for copy in swaps:
            copy.wait_recv()
        fill(1, halves[0], halves[1])

    work = dict(send=send_out, left=await_left, load=load, rows=first_stage, cross=swap_out, swap=swap_in, chip=chip_sum, act=last_stage)
    for step, k in STEPS:
        work[step](k)

    def grads(e, carry):
        tok, grad = rows[e, :, :width], rows[e, :, width:]
        h = hid[e]
        dg[e] = lax.dot_general(tok, h[:, ff : 2 * ff], first, preferred_element_type=F32)
        du[e] = lax.dot_general(tok, h[:, 2 * ff :], first, preferred_element_type=F32)
        dd[e] = lax.dot_general(grad, h[:, :ff], first, preferred_element_type=F32)
        return carry

    lax.fori_loop(0, half, grads, 0)

    def combine(s):
        picks = [jnp.where(p, 1.0, 0.0) for p in placed(s)]
        out = 0.0
        for k in range(TOPK):
            gate = jnp.sum(
                jnp.where(row_ids == col_ids, meta[s, TOPK + k : TOPK + k + 1, :], 0.0),
                axis=1,
                keepdims=True,
            )
            picked = lax.dot_general(
                picks[k].astype(BF16), ret[s, 0], first, preferred_element_type=F32
            )
            out = out + gate * picked
        grad = lax.dot_general(
            sum(picks).astype(BF16), ret[s, 1], first, preferred_element_type=F32
        )
        return out.astype(BF16), grad.astype(BF16)

    fin_copy = [swap_copy(3 + i, fin_send.at[i], fin_recv.at[i]) for i in range(2)]
    for s in (1, 0):
        for g, i in members:
            out_wait(g, i, s)
        out, grad = combine(s)
        if s == 1:
            fin_send[0] = out
            fin_send[1] = grad
            for copy in fin_copy:
                copy.start()
            lax.fori_loop(half, el, grads, 0)
        else:
            layer_ref[:, cols(x_me, wide)] = out
            igrad_ref[:, cols(x_me, wide)] = grad
    for copy in swaps:
        copy.wait_send()
    for k in range(4):
        for i in range(len(GROUPS[k])):
            for s in range(2):
                for j in range(2):
                    if (k, i, s) not in left and (s or not home(k, i, j)):
                        in_copy(k, i, s, j).wait_send()
                    if not home(k, i, j):
                        out_copy(k, i, s, j).wait_send()
        for h in range(2):
            core_copy[k, h].wait_send()
            far_copy[k, h].wait_send()
            hid_copy[k, h].wait_send()

    for copy in fin_copy:
        copy.wait()
    layer_ref[:, cols(1 - x_me, wide)] = fin_recv[0]
    igrad_ref[:, cols(1 - x_me, wide)] = fin_recv[1]


def store_kernel(layer, igrad, dg, du, dd, layer_out, igrad_out, dg_out, du_out, dd_out, sem):
    pairs = [(dg, dg_out), (du, du_out), (dd, dd_out)]
    pairs = [(layer, layer_out), (igrad, igrad_out)] + pairs
    copies = [pltpu.make_async_copy(src, dst, sem.at[i]) for i, (src, dst) in enumerate(pairs)]
    for copy in copies:
        copy.start()
    for copy in copies:
        copy.wait()


def shards(tokens, routes, gate_values, cotangent, gating_weight, upward_weight, down_weight):
    n_expert, n_dp = lax.axis_size("expert"), lax.axis_size("dp")
    el, width, ff = gating_weight.shape
    row_count = tokens.shape[0]
    per = n_expert * n_dp // 4
    msg = el * CAP
    part = per * CAP
    slots = 4 * part
    half = el // 2
    wide = 3 * ff
    spot = np.arange(per * msg)
    e, s, c = spot // part, spot % part // CAP, spot % CAP
    perm = np.zeros((per * msg, per * msg), np.float32)
    perm[spot, s * msg + e * CAP + c] = 1.0
    hbm = pl.BlockSpec(memory_space=pltpu.HBM)
    vmem = pl.BlockSpec(memory_space=pltpu.VMEM)
    weight_shape = gating_weight.shape
    layer_output, input_grad, dg, du, dd = pl.pallas_call(
        functools.partial(plane_kernel, n_expert, n_dp, el, width),
        out_shape=(
            pltpu.VMEM(tokens.shape, BF16),
            pltpu.VMEM(tokens.shape, BF16),
            pltpu.VMEM(weight_shape, F32),
            pltpu.VMEM(weight_shape, F32),
            pltpu.VMEM(weight_shape, F32),
        ),
        in_specs=[hbm] * 9,
        out_specs=[vmem] * 5,
        scratch_shapes=[
            pltpu.VMEM(tokens.shape, BF16),
            pltpu.VMEM(tokens.shape, BF16),
            pltpu.VMEM((TOPK, row_count), jnp.int32),
            pltpu.VMEM((TOPK, row_count), F32),
            pltpu.VMEM(perm.shape, BF16),
            pltpu.VMEM(perm.shape, BF16),
            pltpu.VMEM(weight_shape, BF16),
            pltpu.VMEM(weight_shape, BF16),
            pltpu.VMEM(weight_shape, BF16),
            pltpu.VMEM((2, row_count, 2 * width), BF16),
            pltpu.VMEM((2, 8, row_count), F32),
            pltpu.VMEM((3, 2, msg, 2 * width), BF16),
            pltpu.VMEM((2, 2, n_expert * msg, 2 * width), BF16),
            pltpu.VMEM((4, per, 2, msg, width), BF16),
            pltpu.VMEM((el, slots, 2 * width), BF16),
            pltpu.VMEM((4, half, part, wide), BF16),
            pltpu.VMEM((4, half, part, wide), F32),
            pltpu.VMEM((4, half, part, wide), BF16),
            pltpu.VMEM((4, half, part, wide), BF16),
            pltpu.VMEM((4, half, part, wide), BF16),
            pltpu.VMEM((el, slots, wide), BF16),
            pltpu.VMEM((2, el, part, width), BF16),
            pltpu.VMEM((4, per, 2, msg, width), BF16),
            pltpu.VMEM((2, 2, n_expert * msg, 2 * width), BF16),
            pltpu.VMEM((2, row_count, 2 * width), BF16),
            pltpu.VMEM((2, row_count, 2 * width), BF16),
            pltpu.SemaphoreType.DMA((4 * per,)),
            pltpu.SemaphoreType.DMA((4 * per,)),
            pltpu.SemaphoreType.DMA((4 * per,)),
            pltpu.SemaphoreType.DMA((4 * per,)),
            pltpu.SemaphoreType.DMA((2, 24)),
            pltpu.SemaphoreType.DMA((2, 5)),
            pltpu.SemaphoreType.DMA((11,)),
        ],
        compiler_params=pltpu.CompilerParams(
            collective_id=0, has_side_effects=True, vmem_limit_bytes=44 * 1024 * 1024
        ),
    )(
        *(
            pltpu.with_memory_space_constraint(a, pltpu.HBM)
            for a in (
                tokens,
                cotangent,
                routes.T,
                gate_values.T,
                jnp.asarray(perm, BF16),
                jnp.asarray(perm.T, BF16),
                gating_weight,
                upward_weight,
                down_weight,
            )
        )
    )
    results = (layer_output, input_grad, dg, du, dd)
    return pl.pallas_call(
        store_kernel,
        out_shape=tuple(jax.ShapeDtypeStruct(r.shape, r.dtype) for r in results),
        in_specs=[vmem] * 5,
        out_specs=[hbm] * 5,
        scratch_shapes=[pltpu.SemaphoreType.DMA((5,))],
        compiler_params=pltpu.CompilerParams(vmem_limit_bytes=16 * 1024 * 1024),
    )(*results)


def general_shards(tokens, routes, gate_values, cotangent, gating_weight, upward_weight, down_weight):
    expert_total = gating_weight.shape[0] * lax.axis_size("expert")
    row_count = tokens.shape[0]
    slot_total = expert_total * CAP
    flat_routes = routes.reshape(-1)
    onehot = (flat_routes[:, None] == jnp.arange(expert_total, dtype=jnp.int32)[None, :]).astype(
        jnp.int32
    )
    position = jnp.sum((jnp.cumsum(onehot, axis=0) - onehot) * onehot, axis=1)
    slot_index = flat_routes * CAP + position
    placed = (slot_index[:, None] == jnp.arange(slot_total, dtype=jnp.int32)[None, :]).astype(
        jnp.float32
    )
    placed = placed.reshape(row_count, TOPK, slot_total)
    selector = jnp.sum(placed, axis=1).astype(jnp.bfloat16)
    slot_gate = jnp.sum(placed * gate_values[:, :, None], axis=(0, 1))
    contract = (((0,), (0,)), ((), ()))
    send_rows = lax.dot_general(selector, tokens, contract, preferred_element_type=jnp.float32)
    send_rows = send_rows.astype(jnp.bfloat16).reshape(expert_total, CAP, -1)
    slot_cotangent = lax.dot_general(
        selector, cotangent, contract, preferred_element_type=jnp.float32
    )
    send_grads = (
        (slot_cotangent * slot_gate[:, None]).astype(jnp.bfloat16).reshape(expert_total, CAP, -1)
    )
    arrived, arrived_grad = (
        lax.all_to_all(send_rows, "expert", split_axis=0, concat_axis=1, tiled=True),
        lax.all_to_all(send_grads, "expert", split_axis=0, concat_axis=1, tiled=True),
    )
    gating, upward, lowering = (
        lax.all_gather(gating_weight, "dp", axis=1, tiled=True),
        lax.all_gather(upward_weight, "dp", axis=1, tiled=True),
        lax.all_gather(down_weight, "dp", axis=1, tiled=True),
    )
    gate_pre = jnp.einsum("erd,edf->erf", arrived, gating, preferred_element_type=jnp.float32)
    up_pre = jnp.einsum("erd,edf->erf", arrived, upward, preferred_element_type=jnp.float32)
    sigmoid_gate = jax.nn.sigmoid(gate_pre)
    activated = gate_pre * sigmoid_gate
    hidden = (activated * up_pre).astype(jnp.bfloat16)
    expert_out = jnp.einsum(
        "erf,edf->erd", hidden, lowering, preferred_element_type=jnp.float32
    ).astype(jnp.bfloat16)
    gating, upward, lowering = (
        lax.all_gather(gating_weight, "dp", axis=1, tiled=True),
        lax.all_gather(upward_weight, "dp", axis=1, tiled=True),
        lax.all_gather(down_weight, "dp", axis=1, tiled=True),
    )
    hidden_grad = jnp.einsum(
        "erd,edf->erf", arrived_grad, lowering, preferred_element_type=jnp.float32
    )
    gate_part = (
        hidden_grad * up_pre * sigmoid_gate * (1.0 + gate_pre * (1.0 - sigmoid_gate))
    ).astype(jnp.bfloat16)
    up_part = (hidden_grad * activated).astype(jnp.bfloat16)
    pair_grad = (
        jnp.einsum("erf,edf->erd", gate_part, gating, preferred_element_type=jnp.float32)
        + jnp.einsum("erf,edf->erd", up_part, upward, preferred_element_type=jnp.float32)
    ).astype(jnp.bfloat16)
    returned_out, returned_grad = (
        lax.all_to_all(expert_out, "expert", split_axis=1, concat_axis=0, tiled=True),
        lax.all_to_all(pair_grad, "expert", split_axis=1, concat_axis=0, tiled=True),
    )
    gating_term = jnp.einsum("erd,erf->edf", arrived, gate_part, preferred_element_type=jnp.float32)
    upward_term = jnp.einsum("erd,erf->edf", arrived, up_part, preferred_element_type=jnp.float32)
    down_term = jnp.einsum("erd,erf->edf", arrived_grad, hidden, preferred_element_type=jnp.float32)
    gating_grad, upward_grad, down_grad = (
        lax.psum_scatter(
            gating_term.astype(jnp.bfloat16), "dp", scatter_dimension=1, tiled=True
        ).astype(jnp.float32),
        lax.psum_scatter(
            upward_term.astype(jnp.bfloat16), "dp", scatter_dimension=1, tiled=True
        ).astype(jnp.float32),
        lax.psum_scatter(
            down_term.astype(jnp.bfloat16), "dp", scatter_dimension=1, tiled=True
        ).astype(jnp.float32),
    )
    returned_flat = returned_out.reshape(slot_total, -1)
    combined = jnp.zeros((row_count, returned_flat.shape[1]), jnp.float32)
    for choice_slot in range(TOPK):
        picker = placed[:, choice_slot, :].astype(jnp.bfloat16)
        picked = jnp.dot(picker, returned_flat, preferred_element_type=jnp.float32)
        combined = combined + gate_values[:, choice_slot][:, None] * picked
    layer_output = combined.astype(jnp.bfloat16)
    input_grad = jnp.dot(
        selector, returned_grad.reshape(slot_total, -1), preferred_element_type=jnp.float32
    ).astype(jnp.bfloat16)
    return (layer_output, input_grad, gating_grad, upward_grad, down_grad)


def solution(mesh):
    n_expert, n_dp = mesh.shape["expert"], mesh.shape["dp"]

    def program(*args):
        el = args[4].shape[0] // n_expert
        width = args[4].shape[1] // n_dp
        part = n_expert * n_dp // 4 * CAP
        fits = (
            n_dp == 4
            and n_expert == sum(map(len, GROUPS))
            and el % 4 == 0
            and el * CAP % 16 == 0
            and part % 16 == 0
            and width % 128 == 0
            and args[4].shape[2] % 128 == 0
            and args[0].shape[0] // (n_expert * n_dp) % 128 == 0
        )
        return jax.shard_map(
            shards if fits else general_shards,
            mesh=mesh,
            in_specs=(
                P(("expert", "dp"), None),
                P(("expert", "dp"), None),
                P(("expert", "dp"), None),
                P(("expert", "dp"), None),
                P("expert", "dp", None),
                P("expert", "dp", None),
                P("expert", "dp", None),
            ),
            out_specs=(
                P(("expert", "dp"), None),
                P(("expert", "dp"), None),
                P("expert", "dp", None),
                P("expert", "dp", None),
                P("expert", "dp", None),
            ),
            check_vma=False,
        )(*args)

    return program
```
